512 devices in a mesh: gx: 64 (over y_lo, z, core), gy: 8 (over x, y_hi).
Axes of the slice: x: 4, y: 4 (y_hi: 2, y_lo: 2; y = y_hi * 2 + y_lo), z: 16, core: 2. Of those that a mesh axis runs over, the one named last changes fastest.
Arguments:
- dist: float32 [19, 8, 256, 1024], P(None, None, 'gx', 'gy'), as said below
- marker_cell: int32 [32768, 128], P(('gx', 'gy')), may hold values from 0 to 3583
- marker_side: int32 [32768, 128], P(('gx', 'gy')), may hold values 0 or 1
- marker_frac: float32 [32768, 128], P(('gx', 'gy')), may hold values from 0 to 1
- blade_vel: float32 [3, 32768, 128], P(None, ('gx', 'gy')), may hold values from -4 to 4
Outputs:
- new_dist: float32 [19, 8, 256, 1024], P(None, None, 'gx', 'gy')
- marker_force: float32 [3, 32768, 128], P(None, ('gx', 'gy'))
The draws below stay inside these ranges and needn't reach their ends.
Inputs may be any that keep to these rules, and one draw needn't show every extreme that they name: `marker_cell`: a cell below the top plane of a tile. `dist`: every distribution is positive.
All inputs are finite; a program needn't handle non-finite values. No bound on the sum of `marker_side` on one device may be relied on, other than what follows from the above.
Results may differ from the reference program's by a relative error of at most 0.0003.
Values sent between devices are 32-bit elements; how exact they have to be, the bound alone decides.
A program may use at most 64 MiB of HBM per device.

```python
import jax
import jax.numpy as jnp
import numpy as np
from jax import lax

NZ = 8
CX = 4
CY = 128
BL_DEV = 64
MK = 128
NX = 256
NY = 1024
BLADES = 32768
N_GX = 64
N_GY = 8


def draw_dist(key, part):
    speeds_x = jnp.asarray(np.array([0, 1, -1, 0, 0, 0, 0, 1, -1, 1, -1, 1, -1, 1, -1, 0, 0, 0, 0]), jnp.float32)
    weights = jnp.asarray(np.array([1.0 / 3.0] + [1.0 / 18.0] * 6 + [1.0 / 36.0] * 12), jnp.float32)
    noise = 0.3 * jax.random.uniform(key, (19, NZ, NX, NY), jnp.float32, -1.0, 1.0)
    shear = 0.08 * (jnp.arange(NZ, dtype=jnp.float32) + 1.0) / NZ
    drift = 3.0 * speeds_x.reshape(19, 1, 1, 1) * shear.reshape(1, NZ, 1, 1)
    return weights.reshape(19, 1, 1, 1) * (1.0 + noise + drift)


def with_ends(entries, own_key, smallest, top_value):
    dims = entries.shape
    place = [jax.random.randint(jax.random.fold_in(own_key, axis), (), 0, dims[axis]) for axis in range(len(dims))]
    entries = entries.at[tuple(place)].set(smallest)
    longest = dims.index(max(dims))
    place[longest] = (place[longest] + 1) % dims[longest]
    return entries.at[tuple(place)].set(top_value)


def level_of(stream_key, extent, cuts, smallest, largest):
    level, own = 1.0, jax.random.fold_in(stream_key, 6)
    for dim, parts in cuts:
        heights = jnp.exp(jax.random.uniform(jax.random.fold_in(own, dim), (parts,), jnp.float32, smallest / len(cuts), largest / len(cuts)))
        level = level * jnp.repeat(heights, extent[dim] // parts).reshape([-1 if axis == dim else 1 for axis in range(len(extent))])
    return level


def gaussian(rng, dims, spread, bound, shards=(), held_as=jnp.bfloat16):
    values = jax.random.normal(rng, dims, jnp.float32) * spread
    if len(shards) > 0:
        values = level_of(rng, dims, shards, -0.22, 0.18) * values
    return jnp.clip(values, min=-bound, max=bound).astype(held_as)


def setup_inputs(seed: int = 0) -> dict:
    keys = jax.random.split(jax.random.key(seed), 6)
    return {
        "dist": draw_dist(jax.random.fold_in(keys[5], 71), 0),
        "marker_cell": with_ends(jax.random.randint(keys[1], (BLADES, MK), 0, (NZ - 1) * CX * CY), jax.random.fold_in(keys[1], 1), 0, ((NZ - 1) * CX * CY) - 1).astype(jnp.int32),
        "marker_side": with_ends((jax.random.randint(keys[2], (BLADES, MK), 0, 3) < 1).astype(jnp.int32), jax.random.fold_in(keys[2], 1), 0, 1),
        "marker_frac": jnp.clip(1.0 * jax.random.uniform(keys[3], (BLADES, MK), jnp.float32) ** level_of(keys[3], (BLADES, MK), ((0, 512),), -0.2, 0.2), 0.0, 1.0),
        "blade_vel": gaussian(keys[4], (3, BLADES, MK), 0.3, 4.0, ((1, 512),), jnp.float32),
    }


VELOCITIES = np.array([[0, 0, 0], [1, 0, 0], [-1, 0, 0], [0, 1, 0], [0, -1, 0], [0, 0, 1], [0, 0, -1],
                       [1, 1, 0], [-1, -1, 0], [1, -1, 0], [-1, 1, 0], [1, 0, 1], [-1, 0, -1], [1, 0, -1],
                       [-1, 0, 1], [0, 1, 1], [0, -1, -1], [0, 1, -1], [0, -1, 1]])
WEIGHTS = np.array([1.0 / 3.0] + [1.0 / 18.0] * 6 + [1.0 / 36.0] * 12)
EXPONENTS = [(0, 0, 0), (1, 0, 0), (0, 1, 0), (0, 0, 1), (2, 0, 0), (0, 2, 0), (0, 0, 2), (1, 1, 0), (0, 1, 1),
             (1, 0, 1), (2, 1, 0), (2, 0, 1), (1, 2, 0), (0, 2, 1), (1, 0, 2), (0, 1, 2), (2, 2, 0), (0, 2, 2), (2, 0, 2)]
RATE_BY_ORDER = [0.0, 0.0, 1.6, 1.2, 1.4]
STIFFNESS = 2.0


def find_index(vector):
    return [position for position in range(19) if list(VELOCITIES[position]) == list(vector)][0]


def opposite_of(index):
    return find_index(-VELOCITIES[index])


def mirror_of(index):
    return find_index([VELOCITIES[index][0], VELOCITIES[index][1], -VELOCITIES[index][2]])


def invert_rows(rows):
    count = len(rows)
    work = [list(rows[row]) + [1.0 if col == row else 0.0 for col in range(count)] for row in range(count)]
    for col in range(count):
        pivot = max(range(col, count), key=lambda row: abs(work[row][col]))
        work[col], work[pivot] = work[pivot], work[col]
        scale = work[col][col]
        work[col] = [value / scale for value in work[col]]
        for row in range(count):
            if row != col:
                factor = work[row][col]
                work[row] = [value - factor * lead for value, lead in zip(work[row], work[col])]
    return [line[count:] for line in work]


def collision_table():
    moment_rows = [[float(vel[0]) ** expo[0] * float(vel[1]) ** expo[1] * float(vel[2]) ** expo[2]
                    for vel in VELOCITIES] for expo in EXPONENTS]
    inverse = invert_rows(moment_rows)
    scaled = [[RATE_BY_ORDER[sum(EXPONENTS[row])] * value for value in moment_rows[row]] for row in range(19)]
    table = [[sum(inverse[row][mid] * scaled[mid][col] for mid in range(19)) for col in range(19)]
             for row in range(19)]
    return np.array(table, dtype=np.float32)


def fluid_moments(dist):
    density = jnp.sum(dist, axis=0)
    momentum = jnp.tensordot(jnp.asarray(VELOCITIES.T, jnp.float32), dist, axes=1, precision=lax.Precision.HIGHEST)
    return density, momentum / density


def collide(dist, density, velocity, force):
    table = jnp.asarray(VELOCITIES, jnp.float32)
    weights = jnp.asarray(WEIGHTS, jnp.float32).reshape(19, 1, 1, 1)
    along = jnp.tensordot(table, velocity, axes=1, precision=lax.Precision.HIGHEST)
    speed_sq = jnp.sum(velocity * velocity, axis=0)
    equil = weights * density * (1.0 + 3.0 * along + 4.5 * along * along - 1.5 * speed_sq)
    offeq = (dist - equil).reshape(19, -1)
    relaxed = jnp.dot(jnp.asarray(collision_table()), offeq, precision=lax.Precision.HIGHEST).reshape(dist.shape)
    pushed = jnp.tensordot(table, force, axes=1, precision=lax.Precision.HIGHEST)
    return dist - relaxed + 3.0 * weights * pushed


def finish_planes(shifted, post):
    result = []
    for index in range(19):
        lift = int(VELOCITIES[index][2])
        moved = shifted[index]
        if lift == 1:
            moved = jnp.concatenate([post[opposite_of(index), :1], moved[:-1]], axis=0)
        elif lift == -1:
            moved = jnp.concatenate([moved[1:], shifted[mirror_of(index)][-1:]], axis=0)
        result.append(moved)
    return jnp.stack(result, axis=0)


def reference(dist, marker_cell, marker_side, marker_frac, blade_vel):
    density, velocity = fluid_moments(dist)
    blade_ids = jnp.arange(BLADES, dtype=jnp.int32) // BL_DEV
    row_x = (blade_ids // N_GY)[:, None]
    row_y = (blade_ids % N_GY)[:, None]
    tile_x = (row_x + marker_side) % N_GX
    plane = marker_cell // (CX * CY)
    within = marker_cell % (CX * CY)
    xpos = within // CY
    ypos = within % CY
    flat = (plane * (NX * NY) + (tile_x * CX + xpos) * NY + row_y * CY + ypos).reshape(-1).astype(jnp.int32)
    vel_flat = velocity.reshape(3, -1)
    lower = jnp.take(vel_flat, flat, axis=1)
    upper = jnp.take(vel_flat, flat + NX * NY, axis=1)
    frac = marker_frac.reshape(-1)
    marker_velocity = (1.0 - frac) * lower + frac * upper
    pushes = STIFFNESS * (blade_vel.reshape(3, -1) - marker_velocity)
    force = jnp.zeros((3, NZ * NX * NY), jnp.float32)
    force = force.at[:, flat].add((1.0 - frac) * pushes).at[:, flat + NX * NY].add(frac * pushes)
    force = force.reshape(3, NZ, NX, NY)
    post = collide(dist, density, velocity, force)
    shifted = [jnp.roll(post[index], (int(VELOCITIES[index][0]), int(VELOCITIES[index][1])), axis=(1, 2))
               for index in range(19)]
    new_dist = finish_planes(shifted, post)
    return new_dist, pushes.reshape(3, BLADES, MK)
```

```python
import jax
import jax.numpy as jnp
from jax import lax
from jax.experimental import pallas as pl
from jax.experimental.pallas import tpu as pltpu
from jax.sharding import PartitionSpec as P

VELOCITIES = [
    (0, 0, 0), (1, 0, 0), (-1, 0, 0), (0, 1, 0), (0, -1, 0), (0, 0, 1), (0, 0, -1),
    (1, 1, 0), (-1, -1, 0), (1, -1, 0), (-1, 1, 0), (1, 0, 1), (-1, 0, -1), (1, 0, -1),
    (-1, 0, 1), (0, 1, 1), (0, -1, -1), (0, 1, -1), (0, -1, 1),
]
WEIGHTS = [1.0 / 3.0] + [1.0 / 18.0] * 6 + [1.0 / 36.0] * 12
RATE2, RATE3, RATE4 = 1.6, 1.2, 1.4
STIFFNESS = 2.0

NZ, TX, TY = 8, 4, 128
BL, MK = 64, 128
CELLS = TX * NZ
F32, BF16 = jnp.float32, jnp.bfloat16
MESH = pl.DeviceIdType.MESH

XP = [i for i in range(19) if VELOCITIES[i][0] == 1]
XN = [i for i in range(19) if VELOCITIES[i][0] == -1]
YP = [i for i in range(19) if VELOCITIES[i][1] == 1]
YN = [i for i in range(19) if VELOCITIES[i][1] == -1]
HOPS = (-1, 0, 1, 2)
PEERS = [(t, s) for t in HOPS for s in (-1, 0, 1) if (t, s) != (0, 0)]


def opposite_of(i):
    return VELOCITIES.index(tuple(-c for c in VELOCITIES[i]))


def mirror_of(i):
    a, b, c = VELOCITIES[i]
    return VELOCITIES.index((a, b, -c))


def momentum_of(f):
    s = [f[2 * p + 1] + f[2 * p + 2] for p in range(9)]
    d = [f[2 * p + 1] - f[2 * p + 2] for p in range(9)]
    pxy, pxz, pyz = s[3] + s[4], s[5] + s[6], s[7] + s[8]
    density = f[0] + s[0] + s[1] + s[2] + pxy + pxz + pyz
    jx = d[0] + (d[3] + d[4]) + (d[5] + d[6])
    jy = d[1] + (d[3] - d[4]) + (d[7] + d[8])
    jz = d[2] + (d[5] - d[6]) + (d[7] - d[8])
    return s, d, density, jx, jy, jz


def collided(f):
    s, d, rho, jx, jy, jz = momentum_of(f)
    inv = 1.0 / rho
    ux, uy, uz = jx * inv, jy * inv, jz * inv
    ax, ay, az = jx * ux, jy * uy, jz * uz
    third, ninth = rho * (1.0 / 3.0), rho * (1.0 / 9.0)
    sixth = (ax + ay + az) * (1.0 / 6.0)
    pxy, pxz, pyz = s[3] + s[4], s[5] + s[6], s[7] + s[8]
    nxx = RATE2 * (s[0] + pxy + pxz - third - ax)
    nyy = RATE2 * (s[1] + pxy + pyz - third - ay)
    nzz = RATE2 * (s[2] + pxz + pyz - third - az)
    nxy = RATE2 * (s[3] - s[4] - jx * uy)
    nxz = RATE2 * (s[5] - s[6] - jx * uz)
    nyz = RATE2 * (s[7] - s[8] - jy * uz)
    tx, ty, tz = jx * (1.0 / 3.0), jy * (1.0 / 3.0), jz * (1.0 / 3.0)
    nxxy = RATE3 * (d[3] - d[4] - ty)
    nxyy = RATE3 * (d[3] + d[4] - tx)
    nxxz = RATE3 * (d[5] - d[6] - tz)
    nxzz = RATE3 * (d[5] + d[6] - tx)
    nyyz = RATE3 * (d[7] - d[8] - tz)
    nyzz = RATE3 * (d[7] + d[8] - ty)
    base = ninth - sixth
    qxy = RATE4 * (pxy - base - 0.5 * (ax + ay))
    qxz = RATE4 * (pxz - base - 0.5 * (ax + az))
    qyz = RATE4 * (pyz - base - 0.5 * (ay + az))
    even = [
        0.5 * (nxx - qxy - qxz), 0.5 * (nyy - qxy - qyz), 0.5 * (nzz - qxz - qyz),
        0.25 * (qxy + nxy), 0.25 * (qxy - nxy),
        0.25 * (qxz + nxz), 0.25 * (qxz - nxz),
        0.25 * (qyz + nyz), 0.25 * (qyz - nyz),
    ]
    odd = [
        -0.5 * (nxyy + nxzz), -0.5 * (nxxy + nyzz), -0.5 * (nxxz + nyyz),
        0.25 * (nxyy + nxxy), 0.25 * (nxyy - nxxy),
        0.25 * (nxzz + nxxz), 0.25 * (nxzz - nxxz),
        0.25 * (nyzz + nyyz), 0.25 * (nyzz - nyyz),
    ]
    out = [f[0] + (nxx + nyy + nzz - qxy - qxz - qyz)]
    for p in range(9):
        out.append(f[2 * p + 1] - (even[p] + odd[p]))
        out.append(f[2 * p + 2] - (even[p] - odd[p]))
    return out


def pushed(i, force):
    total = None
    for c, part in zip(VELOCITIES[i], force):
        if c != 0:
            term = part if c > 0 else -part
            total = term if total is None else total + term
    return None if total is None else (3.0 * WEIGHTS[i]) * total


def kernel(dist_h, cell_h, side_h, frac_h, blade_h, new_h, mf_h,
           dist_v, cell_v, side_v, frac_v, blade_v, new_v, mf_v,
           vel_n, vel_f, near_v, post_v, xs_p, xs_n, xr_m, xr_p,
           e_v, er_m1, er_m2, er_p1, ys_p, ys_n, yr_p, yr_n,
           in_sem, out_sem, v_sem, x_sem, e_sem, yp_sem, yn_sem):
    n_gx, n_gy = lax.axis_size("gx"), lax.axis_size("gy")
    gx, gy = lax.axis_index("gx"), lax.axis_index("gy")

    def peer(t, s):
        return (lax.rem(gx + t + n_gx, n_gx), lax.rem(gy + s + n_gy, n_gy))

    def remote(src, dst, sems, slot, t, s):
        return pltpu.make_async_remote_copy(
            src_ref=src, dst_ref=dst, send_sem=sems.at[0, slot], recv_sem=sems.at[1, slot],
            device_id=peer(t, s), device_id_type=MESH)

    loads = [pltpu.make_async_copy(h, v, in_sem.at[n]) for n, (h, v) in enumerate(
        ((dist_h, dist_v), (cell_h, cell_v), (side_h, side_v), (frac_h, frac_v), (blade_h, blade_v)))]
    for load in loads:
        load.start()
    barrier = pltpu.get_barrier_semaphore()
    for t, s in PEERS:
        pl.semaphore_signal(barrier, inc=1, device_id=peer(-t, -s), device_id_type=MESH)

    def rows(x):
        return pl.ds(x * NZ, NZ)

    def planes(x):
        return pl.ds(x, NZ, stride=TX)

    loads[0].wait()
    for x in range(TX):
        _, _, rho, jx, jy, jz = momentum_of([dist_v[i, planes(x), :] for i in range(19)])
        inv = 1.0 / rho
        for c, j in enumerate((jx, jy, jz)):
            vel_n[c, rows(x), :] = j * inv

    pl.semaphore_wait(barrier, len(PEERS))
    send_vel = remote(vel_n, vel_f, v_sem, 0, -1, 0)
    send_vel.start()

    for x in range(TX):
        post = collided([dist_v[i, planes(x), :] for i in range(19)])
        for i in range(19):
            post_v[i, rows(x), :] = post[i]
        if x == 0:
            for n, i in enumerate(XN):
                xs_n[n] = post[i]
        if x == TX - 1:
            for n, i in enumerate(XP):
                xs_p[n] = post[i]
    send_x = [remote(xs_p, xr_m, x_sem, 0, 1, 0), remote(xs_n, xr_p, x_sem, 1, -1, 0)]
    for copy in send_x:
        copy.start()

    lane = lax.broadcasted_iota(jnp.int32, (NZ, TY), 1)
    plane = lax.broadcasted_iota(jnp.int32, (NZ, TY), 0)

    def packed(blocks, column):
        total = None
        for n, block in enumerate(blocks):
            part = jnp.where(lane == plane + n * NZ, jnp.broadcast_to(block[:, column:column + 1], (NZ, TY)), 0.0)
            total = part if total is None else total + part
        return jnp.sum(total, axis=0, keepdims=True)

    for n, i in enumerate(YP):
        ys_p[3 + n:4 + n, :] = packed([post_v[i, rows(x), :] for x in range(TX)], TY - 1)
    for n, i in enumerate(YN):
        ys_n[3 + n:4 + n, :] = packed([post_v[i, rows(x), :] for x in range(TX)], 0)

    for load in loads[1:]:
        load.wait()

    def place(b):
        cell = cell_v[pl.ds(b * 8, 8), :]
        spot = cell & (TY - 1)
        row = ((cell >> 7) & (TX - 1)) * NZ + (cell >> 9)
        return spot, row

    def interpolated(table, b):
        spot, row = place(b)
        frac = frac_v[pl.ds(b * 8, 8), :]
        rest = 1.0 - frac
        total = [jnp.zeros((8, MK), F32) for _ in range(3)]
        for r in range(CELLS):
            weight = jnp.where(row == r, rest, jnp.where(row == r - 1, frac, 0.0))
            for c in range(3):
                line = jnp.broadcast_to(table[c, r:r + 1, :], (8, TY))
                total[c] = total[c] + weight * jnp.take_along_axis(line, spot, axis=1)
        return total

    def near_step(b, carry):
        found = interpolated(vel_n, b)
        for c in range(3):
            near_v[c, pl.ds(b * 8, 8), :] = found[c]
        return carry

    lax.fori_loop(0, BL // 8, near_step, 0, unroll=4)

    spots = lax.broadcasted_iota(jnp.int32, (TY, MK), 0).astype(F32).astype(BF16)
    lines = lax.broadcasted_iota(jnp.int32, (CELLS, MK), 0).astype(F32).astype(BF16)
    one, zero = jnp.ones((), BF16), jnp.zeros((), BF16)

    def spread(x, j, n):
        return jnp.broadcast_to(x[j:j + 1, :], (n, MK))

    def scatter(side, force_of):
        def step(b, total):
            spot, row = place(b)
            spot, row = spot.astype(F32).astype(BF16), row.astype(F32).astype(BF16)
            frac = frac_v[pl.ds(b * 8, 8), :]
            here = side_v[pl.ds(b * 8, 8), :] == side
            force = force_of(b)
            parts = []
            for c in range(3):
                own = jnp.where(here, force[c], 0.0)
                for value in ((1.0 - frac) * own, frac * own):
                    high = value.astype(BF16)
                    parts.append((high, (value - high.astype(F32)).astype(BF16)))
            hot = jnp.concatenate(
                [jnp.where(spots == spread(spot, j, TY), one, zero) for j in range(8)], axis=1)
            blocks = []
            for c in range(3):
                for h in range(2):
                    blocks.append(jnp.concatenate([
                        jnp.where(lines == spread(row, j, CELLS), spread(parts[2 * c][h], j, CELLS),
                                  jnp.where(lines == spread(row, j, CELLS) + 1,
                                            spread(parts[2 * c + 1][h], j, CELLS), zero))
                        for j in range(8)], axis=1))
            return total + lax.dot_general(jnp.concatenate(blocks, axis=0), hot, (((1,), (1,)), ((), ())),
                                           preferred_element_type=F32)
        total = lax.fori_loop(0, BL // 8, step, jnp.zeros((6 * CELLS, TY), F32), unroll=8)
        for c in range(3):
            e_v[c, side * CELLS:(side + 1) * CELLS, :] = (
                total[2 * c * CELLS:(2 * c + 1) * CELLS] + total[(2 * c + 1) * CELLS:(2 * c + 2) * CELLS])

    def near_force(b):
        return [STIFFNESS * (blade_v[c, pl.ds(b * 8, 8), :] - near_v[c, pl.ds(b * 8, 8), :]) for c in range(3)]

    scatter(0, near_force)

    send_vel.wait()

    def far_force(b):
        here = side_v[pl.ds(b * 8, 8), :] == 1
        found = interpolated(vel_f, b)
        force = []
        for c in range(3):
            vel = jnp.where(here, found[c], near_v[c, pl.ds(b * 8, 8), :])
            force.append(STIFFNESS * (blade_v[c, pl.ds(b * 8, 8), :] - vel))
            mf_v[c, pl.ds(b * 8, 8), :] = force[c]
        return force

    scatter(1, far_force)

    send_e = [remote(e_v.at[:, 3 * NZ:8 * NZ, :], er_m1, e_sem, 0, 1, 0),
              remote(e_v.at[:, 7 * NZ:8 * NZ, :], er_m2, e_sem, 1, 2, 0),
              remote(e_v.at[:, 0:NZ, :], er_p1, e_sem, 2, -1, 0)]
    for copy in send_e:
        copy.start()
    for c in range(3):
        blocks = [e_v[c, rows(x), :] for x in range(2 * TX)]
        ys_p[c:c + 1, :] = packed(blocks, TY - 1)
        ys_n[c:c + 1, :] = packed(blocks, 0)
    send_y = []
    for n, t in enumerate(HOPS):
        send_y.append(remote(ys_p, yr_p.at[n], yp_sem, n, t, 1))
        send_y.append(remote(ys_n, yr_n.at[n], yn_sem, n, t, -1))
    for copy in send_y:
        copy.start()
    store_mf = pltpu.make_async_copy(mf_v, mf_h, out_sem.at[0])
    store_mf.start()

    for copy in send_x + send_e + send_y:
        copy.wait()

    force = {}
    for x in range(-1, TX + 1):
        both = []
        for c in range(3):
            total = er_m1[c, pl.ds((x + 1) * NZ, NZ), :] if x < TX else er_p1[c]
            if x == -1:
                total = total + er_m2[c]
            else:
                total = total + e_v[c, rows(x), :]
            both.append(total)
        force[x] = both

    def edge(ref, group):
        total = None
        for n, t in enumerate(HOPS):
            part = pltpu.roll(ref[n], (NZ - NZ * TX * t) % TY, 1)
            total = part if total is None else total + part
        sides = [total[c:c + 1, :] for c in range(3)]
        return {i: total[3 + n:4 + n, :] + pushed(i, sides) for n, i in enumerate(group)}

    edges = edge(yr_p, YP)
    edges.update(edge(yr_n, YN))

    def post_at(i, x):
        if x == -1:
            value = xr_m[XP.index(i)]
        elif x == TX:
            value = xr_p[XN.index(i)]
        else:
            value = post_v[i, rows(x), :]
        push = pushed(i, force[x])
        return value if push is None else value + push

    def moved(i, x):
        value = post_at(i, x)
        cy = VELOCITIES[i][1]
        if cy == 0:
            return value
        column = jnp.sum(jnp.where(lane == plane + (x + 1) * NZ, jnp.broadcast_to(edges[i], (NZ, TY)), 0.0),
                         axis=1, keepdims=True)
        turned = pltpu.roll(value, cy % TY, 1)
        return jnp.where(lane == (0 if cy == 1 else TY - 1), jnp.broadcast_to(column, (NZ, TY)), turned)

    for x in range(TX):
        for i in range(19):
            cx, _, cz = VELOCITIES[i]
            value = moved(i, x - cx)
            if cz == 1:
                value = jnp.where(plane == 0, post_at(opposite_of(i), x), pltpu.roll(value, 1, 0))
            elif cz == -1:
                value = jnp.where(plane == NZ - 1, moved(mirror_of(i), x - cx), pltpu.roll(value, NZ - 1, 0))
            new_v[i, planes(x), :] = value

    store_new = pltpu.make_async_copy(new_v, new_h, out_sem.at[1])
    store_new.start()
    store_mf.wait()
    store_new.wait()


def local(dist, marker_cell, marker_side, marker_frac, blade_vel):
    hbm = pl.BlockSpec(memory_space=pl.ANY)
    field = pltpu.VMEM((3, CELLS, TY), F32)
    marks = pltpu.VMEM((3, BL, MK), F32)
    block = pltpu.VMEM((5, NZ, TY), F32)
    edge = pltpu.VMEM((8, TY), F32)
    dma = pltpu.SemaphoreType.DMA
    new, force = pl.pallas_call(
        kernel,
        out_shape=(jax.ShapeDtypeStruct((19, CELLS, TY), F32), jax.ShapeDtypeStruct((3, BL, MK), F32)),
        in_specs=[hbm] * 5,
        out_specs=(hbm, hbm),
        scratch_shapes=[
            pltpu.VMEM((19, CELLS, TY), F32), pltpu.VMEM((BL, MK), jnp.int32), pltpu.VMEM((BL, MK), jnp.int32),
            pltpu.VMEM((BL, MK), F32), marks, pltpu.VMEM((19, CELLS, TY), F32), marks,
            field, field, marks, pltpu.VMEM((19, CELLS, TY), F32), block, block, block, block,
            pltpu.VMEM((3, 2 * CELLS, TY), F32), pltpu.VMEM((3, 5 * NZ, TY), F32),
            pltpu.VMEM((3, NZ, TY), F32), pltpu.VMEM((3, NZ, TY), F32),
            edge, edge, pltpu.VMEM((4, 8, TY), F32), pltpu.VMEM((4, 8, TY), F32),
            dma((5,)), dma((2,)), dma((2, 1)), dma((2, 2)), dma((2, 3)), dma((2, 4)), dma((2, 4)),
        ],
        compiler_params=pltpu.CompilerParams(collective_id=0, has_side_effects=True),
        name="canopy_step",
    )(dist.reshape(19, CELLS, TY), marker_cell, marker_side, marker_frac, blade_vel)
    return new.reshape(dist.shape), force


def solution(mesh):
    return jax.shard_map(
        local,
        mesh=mesh,
        in_specs=(
            P(None, None, "gx", "gy"),
            P(("gx", "gy"), None),
            P(("gx", "gy"), None),
            P(("gx", "gy"), None),
            P(None, ("gx", "gy"), None),
        ),
        out_specs=(P(None, None, "gx", "gy"), P(None, ("gx", "gy"), None)),
        check_vma=False,
    )
```

```python
import jax
import jax.numpy as jnp
from jax import lax
from jax.experimental import pallas as pl
from jax.experimental.pallas import tpu as pltpu
from jax.sharding import PartitionSpec as P

VELOCITIES = [
    (0, 0, 0), (1, 0, 0), (-1, 0, 0), (0, 1, 0), (0, -1, 0), (0, 0, 1), (0, 0, -1),
    (1, 1, 0), (-1, -1, 0), (1, -1, 0), (-1, 1, 0), (1, 0, 1), (-1, 0, -1), (1, 0, -1),
    (-1, 0, 1), (0, 1, 1), (0, -1, -1), (0, 1, -1), (0, -1, 1),
]
WEIGHTS = [1.0 / 3.0] + [1.0 / 18.0] * 6 + [1.0 / 36.0] * 12
RATE2, RATE3, RATE4 = 1.6, 1.2, 1.4
STIFFNESS = 2.0

NZ, TX, TY = 8, 4, 128
BL, MK = 64, 128
CELLS = TX * NZ
F32, BF16 = jnp.float32, jnp.bfloat16
MESH = pl.DeviceIdType.MESH

XP = [i for i in range(19) if VELOCITIES[i][0] == 1]
XN = [i for i in range(19) if VELOCITIES[i][0] == -1]
YP = [i for i in range(19) if VELOCITIES[i][1] == 1]
YN = [i for i in range(19) if VELOCITIES[i][1] == -1]
HOPS = (-1, 0, 1, 2)
PEERS = [(t, s) for t in HOPS for s in (-1, 0, 1) if (t, s) != (0, 0)]


def opposite_of(i):
    return VELOCITIES.index(tuple(-c for c in VELOCITIES[i]))


def mirror_of(i):
    a, b, c = VELOCITIES[i]
    return VELOCITIES.index((a, b, -c))


def momentum_of(f):
    s = [f[2 * p + 1] + f[2 * p + 2] for p in range(9)]
    d = [f[2 * p + 1] - f[2 * p + 2] for p in range(9)]
    pxy, pxz, pyz = s[3] + s[4], s[5] + s[6], s[7] + s[8]
    density = f[0] + s[0] + s[1] + s[2] + pxy + pxz + pyz
    jx = d[0] + (d[3] + d[4]) + (d[5] + d[6])
    jy = d[1] + (d[3] - d[4]) + (d[7] + d[8])
    jz = d[2] + (d[5] - d[6]) + (d[7] - d[8])
    return s, d, density, jx, jy, jz


def collided(f):
    s, d, rho, jx, jy, jz = momentum_of(f)
    inv = 1.0 / rho
    ux, uy, uz = jx * inv, jy * inv, jz * inv
    ax, ay, az = jx * ux, jy * uy, jz * uz
    third, ninth = rho * (1.0 / 3.0), rho * (1.0 / 9.0)
    sixth = (ax + ay + az) * (1.0 / 6.0)
    pxy, pxz, pyz = s[3] + s[4], s[5] + s[6], s[7] + s[8]
    nxx = RATE2 * (s[0] + pxy + pxz - third - ax)
    nyy = RATE2 * (s[1] + pxy + pyz - third - ay)
    nzz = RATE2 * (s[2] + pxz + pyz - third - az)
    nxy = RATE2 * (s[3] - s[4] - jx * uy)
    nxz = RATE2 * (s[5] - s[6] - jx * uz)
    nyz = RATE2 * (s[7] - s[8] - jy * uz)
    tx, ty, tz = jx * (1.0 / 3.0), jy * (1.0 / 3.0), jz * (1.0 / 3.0)
    nxxy = RATE3 * (d[3] - d[4] - ty)
    nxyy = RATE3 * (d[3] + d[4] - tx)
    nxxz = RATE3 * (d[5] - d[6] - tz)
    nxzz = RATE3 * (d[5] + d[6] - tx)
    nyyz = RATE3 * (d[7] - d[8] - tz)
    nyzz = RATE3 * (d[7] + d[8] - ty)
    base = ninth - sixth
    qxy = RATE4 * (pxy - base - 0.5 * (ax + ay))
    qxz = RATE4 * (pxz - base - 0.5 * (ax + az))
    qyz = RATE4 * (pyz - base - 0.5 * (ay + az))
    even = [
        0.5 * (nxx - qxy - qxz), 0.5 * (nyy - qxy - qyz), 0.5 * (nzz - qxz - qyz),
        0.25 * (qxy + nxy), 0.25 * (qxy - nxy),
        0.25 * (qxz + nxz), 0.25 * (qxz - nxz),
        0.25 * (qyz + nyz), 0.25 * (qyz - nyz),
    ]
    odd = [
        -0.5 * (nxyy + nxzz), -0.5 * (nxxy + nyzz), -0.5 * (nxxz + nyyz),
        0.25 * (nxyy + nxxy), 0.25 * (nxyy - nxxy),
        0.25 * (nxzz + nxxz), 0.25 * (nxzz - nxxz),
        0.25 * (nyzz + nyyz), 0.25 * (nyzz - nyyz),
    ]
    out = [f[0] + (nxx + nyy + nzz - qxy - qxz - qyz)]
    for p in range(9):
        out.append(f[2 * p + 1] - (even[p] + odd[p]))
        out.append(f[2 * p + 2] - (even[p] - odd[p]))
    return out


def pushed(i, force):
    total = None
    for c, part in zip(VELOCITIES[i], force):
        if c != 0:
            term = part if c > 0 else -part
            total = term if total is None else total + term
    return None if total is None else (3.0 * WEIGHTS[i]) * total


def rows(x):
    return pl.ds(x * NZ, NZ)


def planes(x):
    return pl.ds(x, NZ, stride=TX)


def lanes_and_planes():
    return (lax.broadcasted_iota(jnp.int32, (NZ, TY), 1), lax.broadcasted_iota(jnp.int32, (NZ, TY), 0))


def packed(blocks, column, first=0):
    lane, plane = lanes_and_planes()
    total = None
    for n, block in enumerate(blocks):
        part = jnp.where(lane == plane + (first + n) * NZ,
                         jnp.broadcast_to(block[:, column:column + 1], (NZ, TY)), 0.0)
        total = part if total is None else total + part
    return jnp.sum(total, axis=0, keepdims=True)


def exchange(dist_h, cell_h, side_h, frac_h, blade_h, new_v, mf_v, yr_p, yr_n,
             dist_v, cell_v, side_v, frac_v, blade_v,
             vel_n, vel_f, near_v, post_v, xs_p, xs_n, xr_m, xr_p,
             e_v, er_m1, er_m2, ys_p, ys_n,
             in_sem, v_sem, x_sem, e_sem, yp_sem, yn_sem):
    n_gx, n_gy = lax.axis_size("gx"), lax.axis_size("gy")
    gx, gy = lax.axis_index("gx"), lax.axis_index("gy")

    def peer(t, s):
        return (lax.rem(gx + t + n_gx, n_gx), lax.rem(gy + s + n_gy, n_gy))

    def remote(src, dst, sems, slot, t, s):
        return pltpu.make_async_remote_copy(
            src_ref=src, dst_ref=dst, send_sem=sems.at[0, slot], recv_sem=sems.at[1, slot],
            device_id=peer(t, s), device_id_type=MESH)

    barrier = pltpu.get_barrier_semaphore()
    for t, s in PEERS:
        pl.semaphore_signal(barrier, inc=1, device_id=peer(-t, -s), device_id_type=MESH)
    loads = [pltpu.make_async_copy(h, v, in_sem.at[n]) for n, (h, v) in enumerate(
        ((dist_h, dist_v), (cell_h, cell_v), (side_h, side_v), (frac_h, frac_v), (blade_h, blade_v)))]
    for load in loads:
        load.start()

    loads[0].wait()
    for x in range(TX):
        _, _, rho, jx, jy, jz = momentum_of([dist_v[i, planes(x), :] for i in range(19)])
        inv = 1.0 / rho
        for c, j in enumerate((jx, jy, jz)):
            vel_n[c, rows(x), :] = j * inv

    pl.semaphore_wait(barrier, len(PEERS))
    send_vel = remote(vel_n, vel_f, v_sem, 0, -1, 0)
    send_vel.start()

    for x in range(TX):
        post = collided([dist_v[i, planes(x), :] for i in range(19)])
        for i in range(19):
            post_v[i, rows(x), :] = post[i]
        if x == 0:
            for n, i in enumerate(XN):
                xs_n[n] = post[i]
        if x == TX - 1:
            for n, i in enumerate(XP):
                xs_p[n] = post[i]
    for n, i in enumerate(YP):
        ys_p[3 + n:4 + n, :] = packed([post_v[i, rows(x), :] for x in range(TX)], TY - 1)
    for n, i in enumerate(YN):
        ys_n[3 + n:4 + n, :] = packed([post_v[i, rows(x), :] for x in range(TX)], 0)

    for load in loads[1:]:
        load.wait()

    def place(b):
        cell = cell_v[pl.ds(b * 8, 8), :]
        spot = cell & (TY - 1)
        row = ((cell >> 7) & (TX - 1)) * NZ + (cell >> 9)
        return spot, row

    def interpolated(table, b):
        spot, row = place(b)
        frac = frac_v[pl.ds(b * 8, 8), :]
        rest = 1.0 - frac
        total = [jnp.zeros((8, MK), F32) for _ in range(3)]
        for r in range(CELLS):
            weight = jnp.where(row == r, rest, jnp.where(row == r - 1, frac, 0.0))
            for c in range(3):
                line = jnp.broadcast_to(table[c, r:r + 1, :], (8, TY))
                total[c] = total[c] + weight * jnp.take_along_axis(line, spot, axis=1)
        return total

    spots = lax.broadcasted_iota(jnp.int32, (TY, MK), 0).astype(F32).astype(BF16)
    lines = lax.broadcasted_iota(jnp.int32, (CELLS, MK), 0).astype(F32).astype(BF16)
    one, zero = jnp.ones((), BF16), jnp.zeros((), BF16)

    def spread(x, j, n):
        return jnp.broadcast_to(x[j:j + 1, :], (n, MK))

    def scatter(side, force_of):
        def step(b, total):
            spot, row = place(b)
            spot, row = spot.astype(F32).astype(BF16), row.astype(F32).astype(BF16)
            frac = frac_v[pl.ds(b * 8, 8), :]
            here = side_v[pl.ds(b * 8, 8), :] == side
            force = force_of(b)
            parts = []
            for c in range(3):
                own = jnp.where(here, force[c], 0.0)
                for value in ((1.0 - frac) * own, frac * own):
                    high = value.astype(BF16)
                    parts.append((high, (value - high.astype(F32)).astype(BF16)))
            hot = jnp.concatenate(
                [jnp.where(spots == spread(spot, j, TY), one, zero) for j in range(8)], axis=1)
            blocks = []
            for c in range(3):
                for h in range(2):
                    blocks.append(jnp.concatenate([
                        jnp.where(lines == spread(row, j, CELLS), spread(parts[2 * c][h], j, CELLS),
                                  jnp.where(lines == spread(row, j, CELLS) + 1,
                                            spread(parts[2 * c + 1][h], j, CELLS), zero))
                        for j in range(8)], axis=1))
            return total + lax.dot_general(jnp.concatenate(blocks, axis=0), hot, (((1,), (1,)), ((), ())),
                                           preferred_element_type=F32)
        total = lax.fori_loop(0, BL // 8, step, jnp.zeros((6 * CELLS, TY), F32), unroll=8)
        for c in range(3):
            e_v[c, side * CELLS:(side + 1) * CELLS, :] = (
                total[2 * c * CELLS:(2 * c + 1) * CELLS] + total[(2 * c + 1) * CELLS:(2 * c + 2) * CELLS])

    def near_force(b):
        found = interpolated(vel_n, b)
        for c in range(3):
            near_v[c, pl.ds(b * 8, 8), :] = found[c]
        return [STIFFNESS * (blade_v[c, pl.ds(b * 8, 8), :] - found[c]) for c in range(3)]

    scatter(0, near_force)
    for c in range(3):
        blocks = [e_v[c, rows(x), :] for x in range(TX)]
        xs_n[5 + c] = blocks[0]
        xs_p[5 + c] = blocks[-1]
        ys_p[c:c + 1, :] = packed(blocks, TY - 1)
        ys_n[c:c + 1, :] = packed(blocks, 0)
    send_x = [remote(xs_p, xr_m, x_sem, 0, 1, 0), remote(xs_n, xr_p, x_sem, 1, -1, 0)]
    for copy in send_x:
        copy.start()

    send_vel.wait()

    def far_force(b):
        here = side_v[pl.ds(b * 8, 8), :] == 1
        found = interpolated(vel_f, b)
        force = []
        for c in range(3):
            vel = jnp.where(here, found[c], near_v[c, pl.ds(b * 8, 8), :])
            force.append(STIFFNESS * (blade_v[c, pl.ds(b * 8, 8), :] - vel))
            mf_v[c, pl.ds(b * 8, 8), :] = force[c]
        return force

    scatter(1, far_force)

    for c in range(3):
        blocks = [e_v[c, rows(x), :] for x in range(TX, 2 * TX)]
        ys_p[c:c + 1, :] = ys_p[c:c + 1, :] + packed(blocks, TY - 1, TX)
        ys_n[c:c + 1, :] = ys_n[c:c + 1, :] + packed(blocks, 0, TX)
    send_y = []
    for n, t in reversed(list(enumerate(HOPS))):
        send_y.append(remote(ys_p, yr_p.at[n], yp_sem, n, t, 1))
        send_y.append(remote(ys_n, yr_n.at[n], yn_sem, n, t, -1))
    for copy in send_y:
        copy.start()
    send_e = [remote(e_v.at[:, CELLS:, :], er_m1, e_sem, 0, 1, 0),
              remote(e_v.at[:, 2 * CELLS - NZ:, :], er_m2, e_sem, 1, 2, 0)]
    for copy in send_e:
        copy.start()

    for copy in send_x + send_e:
        copy.wait()

    force = {-1: [er_m2[c] + xr_m[5 + c] for c in range(3)],
             TX: [e_v[c, rows(TX), :] + xr_p[5 + c] for c in range(3)]}
    for x in range(TX):
        force[x] = [e_v[c, rows(x), :] + er_m1[c, rows(x), :] for c in range(3)]

    _, plane = lanes_and_planes()

    def post_at(i, x):
        if x == -1:
            value = xr_m[XP.index(i)]
        elif x == TX:
            value = xr_p[XN.index(i)]
        else:
            value = post_v[i, rows(x), :]
        push = pushed(i, force[x])
        return value if push is None else value + push

    def moved(i, x):
        value = post_at(i, x)
        cy = VELOCITIES[i][1]
        return value if cy == 0 else pltpu.roll(value, cy % TY, 1)

    for x in range(TX):
        for i in range(19):
            cx, _, cz = VELOCITIES[i]
            value = moved(i, x - cx)
            if cz == 1:
                value = jnp.where(plane == 0, post_at(opposite_of(i), x), pltpu.roll(value, 1, 0))
            elif cz == -1:
                value = jnp.where(plane == NZ - 1, moved(mirror_of(i), x - cx), pltpu.roll(value, NZ - 1, 0))
            new_v[i, planes(x), :] = value

    for copy in send_y:
        copy.wait()


def finish(mid, mf, yr_p, yr_n, new_h, mf_h, new_v, sem):
    straight = [i for i in range(19) if VELOCITIES[i][1] == 0]
    copies = [pltpu.make_async_copy(mid.at[i], new_h.at[i], sem.at[i]) for i in straight]
    copies.append(pltpu.make_async_copy(mf, mf_h, sem.at[19]))
    for copy in copies:
        copy.start()
    lane, plane = lanes_and_planes()

    def edge(ref, group):
        total = None
        for n, t in enumerate(HOPS):
            part = pltpu.roll(ref[n], (NZ - NZ * TX * t) % TY, 1)
            total = part if total is None else total + part
        sides = [total[c:c + 1, :] for c in range(3)]
        return {i: total[3 + n:4 + n, :] + pushed(i, sides) for n, i in enumerate(group)}

    edges = edge(yr_p, YP)
    edges.update(edge(yr_n, YN))

    def column(i, x):
        spot = lane == plane + (x + 1) * NZ
        return jnp.broadcast_to(
            jnp.sum(jnp.where(spot, jnp.broadcast_to(edges[i], (NZ, TY)), 0.0), axis=1, keepdims=True), (NZ, TY))

    for i in YP + YN:
        cx, cy, cz = VELOCITIES[i]
        last = 0 if cy == 1 else TY - 1
        for x in range(TX):
            value = column(i, x - cx)
            if cz == 1:
                value = pltpu.roll(value, 1, 0)
                here = jnp.logical_and(lane == last, plane > 0)
            elif cz == -1:
                value = jnp.where(plane == NZ - 1, column(mirror_of(i), x - cx), pltpu.roll(value, NZ - 1, 0))
                here = lane == last
            else:
                here = lane == last
            new_v[i, planes(x), :] = jnp.where(here, value, mid[i, planes(x), :])
        copy = pltpu.make_async_copy(new_v.at[i], new_h.at[i], sem.at[i])
        copy.start()
        copies.append(copy)
    for copy in copies:
        copy.wait()


def local(dist, marker_cell, marker_side, marker_frac, blade_vel):
    hbm = pl.BlockSpec(memory_space=pltpu.HBM)
    vmem = pl.BlockSpec(memory_space=pltpu.VMEM)
    cells = pltpu.VMEM((19, CELLS, TY), F32)
    field = pltpu.VMEM((3, CELLS, TY), F32)
    marks = pltpu.VMEM((3, BL, MK), F32)
    block = pltpu.VMEM((8, NZ, TY), F32)
    edge = pltpu.VMEM((8, TY), F32)
    dma = pltpu.SemaphoreType.DMA
    shape = jax.ShapeDtypeStruct
    mid, mf, yr_p, yr_n = pl.pallas_call(
        exchange,
        out_shape=(shape((19, CELLS, TY), F32), shape((3, BL, MK), F32), shape((4, 8, TY), F32), shape((4, 8, TY), F32)),
        in_specs=[hbm] * 5,
        out_specs=(vmem,) * 4,
        scratch_shapes=[
            cells, pltpu.VMEM((BL, MK), jnp.int32), pltpu.VMEM((BL, MK), jnp.int32), pltpu.VMEM((BL, MK), F32), marks,
            field, field, marks, cells, block, block, block, block,
            pltpu.VMEM((3, 2 * CELLS, TY), F32), field, pltpu.VMEM((3, NZ, TY), F32), edge, edge,
            dma((5,)), dma((2, 1)), dma((2, 2)), dma((2, 2)), dma((2, 4)), dma((2, 4)),
        ],
        compiler_params=pltpu.CompilerParams(collective_id=0, has_side_effects=True, vmem_limit_bytes=32 * 2**20),
        name="exchange",
    )(*(pltpu.with_memory_space_constraint(a, pltpu.HBM) for a in (dist.reshape(19, CELLS, TY), marker_cell, marker_side, marker_frac, blade_vel)))
    new, force = pl.pallas_call(
        finish,
        out_shape=(shape((19, CELLS, TY), F32), shape((3, BL, MK), F32)),
        in_specs=[vmem] * 4,
        out_specs=(hbm, hbm),
        scratch_shapes=[cells, dma((20,))],
        compiler_params=pltpu.CompilerParams(vmem_limit_bytes=16 * 2**20),
        name="finish",
    )(mid, mf, yr_p, yr_n)
    return new.reshape(dist.shape), force


def solution(mesh):
    return jax.shard_map(
        local,
        mesh=mesh,
        in_specs=(
            P(None, None, "gx", "gy"),
            P(("gx", "gy"), None),
            P(("gx", "gy"), None),
            P(("gx", "gy"), None),
            P(None, ("gx", "gy"), None),
        ),
        out_specs=(P(None, None, "gx", "gy"), P(None, ("gx", "gy"), None)),
        check_vma=False,
    )
```

```python
import jax
import jax.numpy as jnp
from jax import lax
from jax.experimental import pallas as pl
from jax.experimental.pallas import tpu as pltpu
from jax.sharding import PartitionSpec as P

VELOCITIES = [
    (0, 0, 0), (1, 0, 0), (-1, 0, 0), (0, 1, 0), (0, -1, 0), (0, 0, 1), (0, 0, -1),
    (1, 1, 0), (-1, -1, 0), (1, -1, 0), (-1, 1, 0), (1, 0, 1), (-1, 0, -1), (1, 0, -1),
    (-1, 0, 1), (0, 1, 1), (0, -1, -1), (0, 1, -1), (0, -1, 1),
]
WEIGHTS = [1.0 / 3.0] + [1.0 / 18.0] * 6 + [1.0 / 36.0] * 12
RATE2, RATE3, RATE4 = 1.6, 1.2, 1.4
STIFFNESS = 2.0

NZ, TX, TY = 8, 4, 128
BL, MK = 64, 128
CELLS = TX * NZ
F32, BF16 = jnp.float32, jnp.bfloat16
MESH = pl.DeviceIdType.MESH

XP = [i for i in range(19) if VELOCITIES[i][0] == 1]
XN = [i for i in range(19) if VELOCITIES[i][0] == -1]
YP = [i for i in range(19) if VELOCITIES[i][1] == 1]
YN = [i for i in range(19) if VELOCITIES[i][1] == -1]
HOPS = (-1, 0, 1, 2)
PEERS = [(t, s) for t in HOPS for s in (-1, 0, 1) if (t, s) != (0, 0)]


def opposite_of(i):
    return VELOCITIES.index(tuple(-c for c in VELOCITIES[i]))


def mirror_of(i):
    a, b, c = VELOCITIES[i]
    return VELOCITIES.index((a, b, -c))


def momentum_of(f):
    s = [f[2 * p + 1] + f[2 * p + 2] for p in range(9)]
    d = [f[2 * p + 1] - f[2 * p + 2] for p in range(9)]
    pxy, pxz, pyz = s[3] + s[4], s[5] + s[6], s[7] + s[8]
    density = f[0] + s[0] + s[1] + s[2] + pxy + pxz + pyz
    jx = d[0] + (d[3] + d[4]) + (d[5] + d[6])
    jy = d[1] + (d[3] - d[4]) + (d[7] + d[8])
    jz = d[2] + (d[5] - d[6]) + (d[7] - d[8])
    return s, d, density, jx, jy, jz


def collided(f):
    s, d, rho, jx, jy, jz = momentum_of(f)
    inv = 1.0 / rho
    ux, uy, uz = jx * inv, jy * inv, jz * inv
    ax, ay, az = jx * ux, jy * uy, jz * uz
    third, ninth = rho * (1.0 / 3.0), rho * (1.0 / 9.0)
    sixth = (ax + ay + az) * (1.0 / 6.0)
    pxy, pxz, pyz = s[3] + s[4], s[5] + s[6], s[7] + s[8]
    nxx = RATE2 * (s[0] + pxy + pxz - third - ax)
    nyy = RATE2 * (s[1] + pxy + pyz - third - ay)
    nzz = RATE2 * (s[2] + pxz + pyz - third - az)
    nxy = RATE2 * (s[3] - s[4] - jx * uy)
    nxz = RATE2 * (s[5] - s[6] - jx * uz)
    nyz = RATE2 * (s[7] - s[8] - jy * uz)
    tx, ty, tz = jx * (1.0 / 3.0), jy * (1.0 / 3.0), jz * (1.0 / 3.0)
    nxxy = RATE3 * (d[3] - d[4] - ty)
    nxyy = RATE3 * (d[3] + d[4] - tx)
    nxxz = RATE3 * (d[5] - d[6] - tz)
    nxzz = RATE3 * (d[5] + d[6] - tx)
    nyyz = RATE3 * (d[7] - d[8] - tz)
    nyzz = RATE3 * (d[7] + d[8] - ty)
    base = ninth - sixth
    qxy = RATE4 * (pxy - base - 0.5 * (ax + ay))
    qxz = RATE4 * (pxz - base - 0.5 * (ax + az))
    qyz = RATE4 * (pyz - base - 0.5 * (ay + az))
    even = [
        0.5 * (nxx - qxy - qxz), 0.5 * (nyy - qxy - qyz), 0.5 * (nzz - qxz - qyz),
        0.25 * (qxy + nxy), 0.25 * (qxy - nxy),
        0.25 * (qxz + nxz), 0.25 * (qxz - nxz),
        0.25 * (qyz + nyz), 0.25 * (qyz - nyz),
    ]
    odd = [
        -0.5 * (nxyy + nxzz), -0.5 * (nxxy + nyzz), -0.5 * (nxxz + nyyz),
        0.25 * (nxyy + nxxy), 0.25 * (nxyy - nxxy),
        0.25 * (nxzz + nxxz), 0.25 * (nxzz - nxxz),
        0.25 * (nyzz + nyyz), 0.25 * (nyzz - nyyz),
    ]
    out = [f[0] + (nxx + nyy + nzz - qxy - qxz - qyz)]
    for p in range(9):
        out.append(f[2 * p + 1] - (even[p] + odd[p]))
        out.append(f[2 * p + 2] - (even[p] - odd[p]))
    return out


def pushed(i, force):
    total = None
    for c, part in zip(VELOCITIES[i], force):
        if c != 0:
            term = part if c > 0 else -part
            total = term if total is None else total + term
    return None if total is None else (3.0 * WEIGHTS[i]) * total


def rows(x):
    return pl.ds(x * NZ, NZ)


def planes(x):
    return pl.ds(x, NZ, stride=TX)


def lanes_and_planes():
    return (lax.broadcasted_iota(jnp.int32, (NZ, TY), 1), lax.broadcasted_iota(jnp.int32, (NZ, TY), 0))


def packed(blocks, column):
    lane, plane = lanes_and_planes()
    total = None
    for n, block in enumerate(blocks):
        part = jnp.where(lane == plane + n * NZ, jnp.broadcast_to(block[:, column:column + 1], (NZ, TY)), 0.0)
        total = part if total is None else total + part
    return jnp.sum(total, axis=0, keepdims=True)


def force_of(fields, vel, axis):
    size = vel[0].shape[axis]
    out = []
    for c in range(3):
        below = pltpu.roll(fields[4] * vel[c], 1, axis)
        above = fields[4] * pltpu.roll(vel[c], size - 1, axis)
        out.append(STIFFNESS * (fields[c] - fields[3] * vel[c] - above - below))
    return out


def exchange(dist_h, cell_h, side_h, frac_h, blade_h, new_v, mf_v, yr_p, yr_n,
             dist_v, cell_v, side_v, frac_v, blade_v,
             vel_n, vel_f, post_v, xs_p, xs_n, xr_m, xr_p,
             g_v, gr_1, gr_2, ys_p, ys_n,
             in_sem, v_sem, x_sem, g_sem, yp_sem, yn_sem):
    n_gx, n_gy = lax.axis_size("gx"), lax.axis_size("gy")
    gx, gy = lax.axis_index("gx"), lax.axis_index("gy")

    def peer(t, s):
        return (lax.rem(gx + t + n_gx, n_gx), lax.rem(gy + s + n_gy, n_gy))

    def remote(src, dst, sems, slot, t, s):
        return pltpu.make_async_remote_copy(
            src_ref=src, dst_ref=dst, send_sem=sems.at[0, slot], recv_sem=sems.at[1, slot],
            device_id=peer(t, s), device_id_type=MESH)

    barrier = pltpu.get_barrier_semaphore()
    for t, s in PEERS:
        pl.semaphore_signal(barrier, inc=1, device_id=peer(-t, -s), device_id_type=MESH)
    loads = [pltpu.make_async_copy(h, v, in_sem.at[n]) for n, (h, v) in enumerate(
        ((cell_h, cell_v), (side_h, side_v), (frac_h, frac_v), (blade_h, blade_v), (dist_h, dist_v)))]
    for load in loads:
        load.start()
    for load in loads:
        load.wait()

    for x in range(TX):
        values = [dist_v[i, planes(x), :] for i in range(19)]
        _, _, rho, jx, jy, jz = momentum_of(values)
        inv = 1.0 / rho
        for c, j in enumerate((jx, jy, jz)):
            vel_n[c, rows(x), :] = j * inv
        for i, post in enumerate(collided(values)):
            post_v[i, rows(x), :] = post

    spots = lax.broadcasted_iota(jnp.int32, (2 * TY, MK), 0).astype(F32).astype(BF16)
    lines = lax.broadcasted_iota(jnp.int32, (CELLS, MK), 0).astype(F32).astype(BF16)
    one, zero = jnp.ones((), BF16), jnp.zeros((), BF16)

    def spread(x, j, n):
        return jnp.broadcast_to(x[j:j + 1, :], (n, MK))

    def place(b):
        cell = cell_v[pl.ds(b * 8, 8), :]
        spot = cell & (TY - 1)
        row = ((cell >> 7) & (TX - 1)) * NZ + (cell >> 9)
        return spot, row

    def halves(value):
        high = value.astype(BF16)
        return high, (value - high.astype(F32)).astype(BF16)

    def scatter_step(b, total):
        spot, row = place(b)
        spot = (spot + side_v[pl.ds(b * 8, 8), :] * TY).astype(F32).astype(BF16)
        row = row.astype(F32).astype(BF16)
        frac = frac_v[pl.ds(b * 8, 8), :]
        rest = 1.0 - frac
        pairs = []
        for c in range(3):
            blade = blade_v[c, pl.ds(b * 8, 8), :]
            pairs.append((halves(rest * blade), halves(frac * blade)))
        pairs.append((halves(rest * rest), halves(frac * frac)))
        pairs.append((halves(rest * frac), None))
        hot = jnp.concatenate([jnp.where(spots == spread(spot, j, 2 * TY), one, zero) for j in range(8)], axis=1)
        blocks = []
        for low, high in pairs:
            for h in range(2):
                parts = []
                for j in range(8):
                    line = spread(row, j, CELLS)
                    upper = zero if high is None else jnp.where(lines == line + 1, spread(high[h], j, CELLS), zero)
                    parts.append(jnp.where(lines == line, spread(low[h], j, CELLS), upper))
                blocks.append(jnp.concatenate(parts, axis=1))
        return total + lax.dot_general(jnp.concatenate(blocks, axis=0), hot, (((1,), (1,)), ((), ())),
                                       preferred_element_type=F32)

    total = lax.fori_loop(0, BL // 8, scatter_step, jnp.zeros((10 * CELLS, 2 * TY), F32), unroll=8)
    for n in range(5):
        both = total[2 * n * CELLS:(2 * n + 1) * CELLS] + total[(2 * n + 1) * CELLS:(2 * n + 2) * CELLS]
        g_v[n, 0:CELLS, :] = both[:, :TY]
        g_v[n, CELLS:2 * CELLS, :] = both[:, TY:]

    ys_p[...] = jnp.zeros_like(ys_p)
    ys_n[...] = jnp.zeros_like(ys_n)
    for n in range(5):
        blocks = [g_v[n, rows(x), :] for x in range(2 * TX)]
        ys_p[n:n + 1, :] = packed(blocks, TY - 1)
        ys_n[n:n + 1, :] = packed(blocks, 0)
    for c in range(3):
        blocks = [vel_n[c, rows(x), :] for x in range(TX)]
        ys_p[5 + c:6 + c, :] = packed(blocks, TY - 1)
        ys_n[5 + c:6 + c, :] = packed(blocks, 0)
    for n in range(5):
        ys_p[8 + n:9 + n, :] = packed([post_v[YP[n], rows(x), :] for x in range(TX)], TY - 1)
        ys_n[8 + n:9 + n, :] = packed([post_v[YN[n], rows(x), :] for x in range(TX)], 0)
    for n in range(5):
        xs_p[n] = post_v[XP[n], rows(TX - 1), :]
        xs_n[n] = post_v[XN[n], rows(0), :]
        xs_p[5 + n] = g_v[n, rows(TX - 1), :]
        xs_n[5 + n] = g_v[n, rows(0), :]
    for c in range(3):
        xs_p[10 + c] = vel_n[c, rows(TX - 1), :]

    pl.semaphore_wait(barrier, len(PEERS))
    send_y = []
    for n, t in reversed(list(enumerate(HOPS))):
        send_y.append(remote(ys_p, yr_p.at[n], yp_sem, n, t, 1))
        send_y.append(remote(ys_n, yr_n.at[n], yn_sem, n, t, -1))
    send_vel = remote(vel_n, vel_f, v_sem, 0, -1, 0)
    send_x = [remote(xs_p, xr_m, x_sem, 0, 1, 0), remote(xs_n, xr_p, x_sem, 1, -1, 0),
              remote(g_v.at[:, 2 * CELLS - NZ:, :], gr_2, g_sem, 1, 2, 0),
              remote(g_v.at[:, CELLS:, :], gr_1, g_sem, 0, 1, 0)]
    for copy in send_y + [send_vel] + send_x:
        copy.start()

    def interpolated(table, b):
        spot, row = place(b)
        frac = frac_v[pl.ds(b * 8, 8), :]
        rest = 1.0 - frac
        found = [jnp.zeros((8, MK), F32) for _ in range(3)]
        for r in range(CELLS):
            weight = jnp.where(row == r, rest, jnp.where(row == r - 1, frac, 0.0))
            for c in range(3):
                line = jnp.broadcast_to(table[c, r:r + 1, :], (8, TY))
                found[c] = found[c] + weight * jnp.take_along_axis(line, spot, axis=1)
        return found

    def near_step(b, carry):
        for c, found in enumerate(interpolated(vel_n, b)):
            mf_v[c, pl.ds(b * 8, 8), :] = STIFFNESS * (blade_v[c, pl.ds(b * 8, 8), :] - found)
        return carry

    def far_step(b, carry):
        far = side_v[pl.ds(b * 8, 8), :] == 1
        for c, found in enumerate(interpolated(vel_f, b)):
            force = STIFFNESS * (blade_v[c, pl.ds(b * 8, 8), :] - found)
            mf_v[c, pl.ds(b * 8, 8), :] = jnp.where(far, force, mf_v[c, pl.ds(b * 8, 8), :])
        return carry

    lax.fori_loop(0, BL // 8, near_step, 0, unroll=4)
    send_vel.wait()
    lax.fori_loop(0, BL // 8, far_step, 0, unroll=4)
    for copy in send_x:
        copy.wait()

    force = {}
    for x in range(-1, TX + 1):
        if x == -1:
            fields = [xr_m[5 + n] + gr_2[n] for n in range(5)]
            vel = [xr_m[10 + c] for c in range(3)]
        elif x == TX:
            fields = [g_v[n, rows(TX), :] + xr_p[5 + n] for n in range(5)]
            vel = [vel_f[c, rows(0), :] for c in range(3)]
        else:
            fields = [g_v[n, rows(x), :] + gr_1[n, rows(x), :] for n in range(5)]
            vel = [vel_n[c, rows(x), :] for c in range(3)]
        force[x] = force_of(fields, vel, 0)

    _, plane = lanes_and_planes()

    def post_at(i, x):
        if x == -1:
            value = xr_m[XP.index(i)]
        elif x == TX:
            value = xr_p[XN.index(i)]
        else:
            value = post_v[i, rows(x), :]
        push = pushed(i, force[x])
        return value if push is None else value + push

    def moved(i, x):
        value = post_at(i, x)
        cy = VELOCITIES[i][1]
        return value if cy == 0 else pltpu.roll(value, cy % TY, 1)

    for x in range(TX):
        for i in range(19):
            cx, _, cz = VELOCITIES[i]
            value = moved(i, x - cx)
            if cz == 1:
                value = jnp.where(plane == 0, post_at(opposite_of(i), x), pltpu.roll(value, 1, 0))
            elif cz == -1:
                value = jnp.where(plane == NZ - 1, moved(mirror_of(i), x - cx), pltpu.roll(value, NZ - 1, 0))
            new_v[i, planes(x), :] = value

    for copy in send_y:
        copy.wait()


def finish(mid, mf, yr_p, yr_n, new_h, mf_h, new_v, sem):
    straight = [i for i in range(19) if VELOCITIES[i][1] == 0]
    copies = [pltpu.make_async_copy(mid.at[i], new_h.at[i], sem.at[i]) for i in straight]
    copies.append(pltpu.make_async_copy(mf, mf_h, sem.at[19]))
    for copy in copies:
        copy.start()
    lane, plane = lanes_and_planes()

    def edge(ref, group):
        total = None
        for n, t in enumerate(HOPS):
            part = pltpu.roll(ref[n], (NZ - NZ * TX * t) % TY, 1)
            total = part if total is None else total + part
        line = [total[n:n + 1, :] for n in range(13)]
        force = force_of(line[:5], line[5:8], 1)
        return {i: line[8 + n] + pushed(i, force) for n, i in enumerate(group)}

    edges = edge(yr_p, YP)
    edges.update(edge(yr_n, YN))

    def column(i, x):
        spot = lane == plane + (x + 1) * NZ
        return jnp.broadcast_to(
            jnp.sum(jnp.where(spot, jnp.broadcast_to(edges[i], (NZ, TY)), 0.0), axis=1, keepdims=True), (NZ, TY))

    for i in YP + YN:
        cx, cy, cz = VELOCITIES[i]
        here = lane == (0 if cy == 1 else TY - 1)
        for x in range(TX):
            value = column(i, x - cx)
            where = here
            if cz == 1:
                value = pltpu.roll(value, 1, 0)
                where = jnp.logical_and(here, plane > 0)
            elif cz == -1:
                value = jnp.where(plane == NZ - 1, column(mirror_of(i), x - cx), pltpu.roll(value, NZ - 1, 0))
            new_v[i, planes(x), :] = jnp.where(where, value, mid[i, planes(x), :])
        copy = pltpu.make_async_copy(new_v.at[i], new_h.at[i], sem.at[i])
        copy.start()
        copies.append(copy)
    for copy in copies:
        copy.wait()


def local(dist, marker_cell, marker_side, marker_frac, blade_vel):
    hbm = pl.BlockSpec(memory_space=pltpu.HBM)
    vmem = pl.BlockSpec(memory_space=pltpu.VMEM)
    cells = pltpu.VMEM((19, CELLS, TY), F32)
    field = pltpu.VMEM((3, CELLS, TY), F32)
    edge = pltpu.VMEM((16, TY), F32)
    dma = pltpu.SemaphoreType.DMA
    shape = jax.ShapeDtypeStruct
    given = [pltpu.with_memory_space_constraint(a, pltpu.HBM) for a in (
        dist.reshape(19, CELLS, TY), marker_cell, marker_side, marker_frac, blade_vel)]
    mid, mf, yr_p, yr_n = pl.pallas_call(
        exchange,
        out_shape=(shape((19, CELLS, TY), F32), shape((3, BL, MK), F32),
                   shape((4, 16, TY), F32), shape((4, 16, TY), F32)),
        in_specs=[hbm] * 5,
        out_specs=(vmem,) * 4,
        scratch_shapes=[
            cells, pltpu.VMEM((BL, MK), jnp.int32), pltpu.VMEM((BL, MK), jnp.int32), pltpu.VMEM((BL, MK), F32),
            pltpu.VMEM((3, BL, MK), F32),
            field, field, cells, pltpu.VMEM((13, NZ, TY), F32), pltpu.VMEM((10, NZ, TY), F32),
            pltpu.VMEM((13, NZ, TY), F32), pltpu.VMEM((10, NZ, TY), F32),
            pltpu.VMEM((5, 2 * CELLS, TY), F32), pltpu.VMEM((5, CELLS, TY), F32), pltpu.VMEM((5, NZ, TY), F32),
            edge, edge,
            dma((5,)), dma((2, 1)), dma((2, 2)), dma((2, 2)), dma((2, 4)), dma((2, 4)),
        ],
        compiler_params=pltpu.CompilerParams(collective_id=0, has_side_effects=True, vmem_limit_bytes=32 * 2**20),
        name="exchange",
    )(*given)
    new, force = pl.pallas_call(
        finish,
        out_shape=(shape((19, CELLS, TY), F32), shape((3, BL, MK), F32)),
        in_specs=[vmem] * 4,
        out_specs=(hbm, hbm),
        scratch_shapes=[cells, dma((20,))],
        compiler_params=pltpu.CompilerParams(vmem_limit_bytes=16 * 2**20),
        name="finish",
    )(mid, mf, yr_p, yr_n)
    return new.reshape(dist.shape), force


def solution(mesh):
    return jax.shard_map(
        local,
        mesh=mesh,
        in_specs=(
            P(None, None, "gx", "gy"),
            P(("gx", "gy"), None),
            P(("gx", "gy"), None),
            P(("gx", "gy"), None),
            P(None, ("gx", "gy"), None),
        ),
        out_specs=(P(None, None, "gx", "gy"), P(None, ("gx", "gy"), None)),
        check_vma=False,
    )
```

```python
import jax
import jax.numpy as jnp
from jax import lax
from jax.experimental import pallas as pl
from jax.experimental.pallas import tpu as pltpu
from jax.sharding import PartitionSpec as P

VELOCITIES = [
    (0, 0, 0), (1, 0, 0), (-1, 0, 0), (0, 1, 0), (0, -1, 0), (0, 0, 1), (0, 0, -1),
    (1, 1, 0), (-1, -1, 0), (1, -1, 0), (-1, 1, 0), (1, 0, 1), (-1, 0, -1), (1, 0, -1),
    (-1, 0, 1), (0, 1, 1), (0, -1, -1), (0, 1, -1), (0, -1, 1),
]
WEIGHTS = [1.0 / 3.0] + [1.0 / 18.0] * 6 + [1.0 / 36.0] * 12
RATE2, RATE3, RATE4 = 1.6, 1.2, 1.4
STIFFNESS = 2.0

NZ, TX, TY = 8, 4, 128
BL, MK = 64, 128
CELLS = TX * NZ
F32, BF16 = jnp.float32, jnp.bfloat16
MESH = pl.DeviceIdType.MESH

XP = [i for i in range(19) if VELOCITIES[i][0] == 1]
XN = [i for i in range(19) if VELOCITIES[i][0] == -1]
YP = [i for i in range(19) if VELOCITIES[i][1] == 1]
YN = [i for i in range(19) if VELOCITIES[i][1] == -1]
HOPS = (-1, 0, 1, 2)
PEERS = [(t, s) for t in HOPS for s in (-1, 0, 1) if (t, s) != (0, 0)]


def opposite_of(i):
    return VELOCITIES.index(tuple(-c for c in VELOCITIES[i]))


def mirror_of(i):
    a, b, c = VELOCITIES[i]
    return VELOCITIES.index((a, b, -c))


def momentum_of(f):
    s = [f[2 * p + 1] + f[2 * p + 2] for p in range(9)]
    d = [f[2 * p + 1] - f[2 * p + 2] for p in range(9)]
    pxy, pxz, pyz = s[3] + s[4], s[5] + s[6], s[7] + s[8]
    density = f[0] + s[0] + s[1] + s[2] + pxy + pxz + pyz
    jx = d[0] + (d[3] + d[4]) + (d[5] + d[6])
    jy = d[1] + (d[3] - d[4]) + (d[7] + d[8])
    jz = d[2] + (d[5] - d[6]) + (d[7] - d[8])
    return s, d, density, jx, jy, jz


def collided(f):
    s, d, rho, jx, jy, jz = momentum_of(f)
    inv = 1.0 / rho
    ux, uy, uz = jx * inv, jy * inv, jz * inv
    ax, ay, az = jx * ux, jy * uy, jz * uz
    third, ninth = rho * (1.0 / 3.0), rho * (1.0 / 9.0)
    sixth = (ax + ay + az) * (1.0 / 6.0)
    pxy, pxz, pyz = s[3] + s[4], s[5] + s[6], s[7] + s[8]
    nxx = RATE2 * (s[0] + pxy + pxz - third - ax)
    nyy = RATE2 * (s[1] + pxy + pyz - third - ay)
    nzz = RATE2 * (s[2] + pxz + pyz - third - az)
    nxy = RATE2 * (s[3] - s[4] - jx * uy)
    nxz = RATE2 * (s[5] - s[6] - jx * uz)
    nyz = RATE2 * (s[7] - s[8] - jy * uz)
    tx, ty, tz = jx * (1.0 / 3.0), jy * (1.0 / 3.0), jz * (1.0 / 3.0)
    nxxy = RATE3 * (d[3] - d[4] - ty)
    nxyy = RATE3 * (d[3] + d[4] - tx)
    nxxz = RATE3 * (d[5] - d[6] - tz)
    nxzz = RATE3 * (d[5] + d[6] - tx)
    nyyz = RATE3 * (d[7] - d[8] - tz)
    nyzz = RATE3 * (d[7] + d[8] - ty)
    base = ninth - sixth
    qxy = RATE4 * (pxy - base - 0.5 * (ax + ay))
    qxz = RATE4 * (pxz - base - 0.5 * (ax + az))
    qyz = RATE4 * (pyz - base - 0.5 * (ay + az))
    even = [
        0.5 * (nxx - qxy - qxz), 0.5 * (nyy - qxy - qyz), 0.5 * (nzz - qxz - qyz),
        0.25 * (qxy + nxy), 0.25 * (qxy - nxy),
        0.25 * (qxz + nxz), 0.25 * (qxz - nxz),
        0.25 * (qyz + nyz), 0.25 * (qyz - nyz),
    ]
    odd = [
        -0.5 * (nxyy + nxzz), -0.5 * (nxxy + nyzz), -0.5 * (nxxz + nyyz),
        0.25 * (nxyy + nxxy), 0.25 * (nxyy - nxxy),
        0.25 * (nxzz + nxxz), 0.25 * (nxzz - nxxz),
        0.25 * (nyzz + nyyz), 0.25 * (nyzz - nyyz),
    ]
    out = [f[0] + (nxx + nyy + nzz - qxy - qxz - qyz)]
    for p in range(9):
        out.append(f[2 * p + 1] - (even[p] + odd[p]))
        out.append(f[2 * p + 2] - (even[p] - odd[p]))
    return out


def pushed(i, force):
    total = None
    for c, part in zip(VELOCITIES[i], force):
        if c != 0:
            term = part if c > 0 else -part
            total = term if total is None else total + term
    return None if total is None else (3.0 * WEIGHTS[i]) * total


def rows(x):
    return pl.ds(x * NZ, NZ)


def planes(x):
    return pl.ds(x, NZ, stride=TX)


def lanes_and_planes():
    return (lax.broadcasted_iota(jnp.int32, (NZ, TY), 1), lax.broadcasted_iota(jnp.int32, (NZ, TY), 0))


def packed(groups, column):
    lane, plane = lanes_and_planes()
    total = None
    for g, blocks in enumerate(groups):
        for n, block in enumerate(blocks):
            part = jnp.where(lane == plane + (g * TX + n) * NZ,
                             jnp.broadcast_to(block[:, column:column + 1], (NZ, TY)), 0.0)
            total = part if total is None else total + part
    return jnp.sum(total, axis=0, keepdims=True)


def force_of(fields, vel, axis):
    size = vel[0].shape[axis]
    out = []
    for c in range(3):
        below = pltpu.roll(fields[4] * vel[c], 1, axis)
        above = fields[4] * pltpu.roll(vel[c], size - 1, axis)
        out.append(STIFFNESS * (fields[c] - fields[3] * vel[c] - above - below))
    return out


def exchange(dist_h, cell_h, side_h, frac_h, blade_h, new_v, mf_v, yr_p, yr_n,
             dist_v, cell_v, side_v, frac_v, blade_v,
             vel_n, vel_f, post_v, xs_p, xs_n, xr_m, xr_p,
             g_v, gf_v, gr_1, gr_2, ys_p, ys_n,
             in_sem, v_sem, x_sem, g_sem, yp_sem, yn_sem):
    n_gx, n_gy = lax.axis_size("gx"), lax.axis_size("gy")
    gx, gy = lax.axis_index("gx"), lax.axis_index("gy")

    def peer(t, s):
        return (lax.rem(gx + t + n_gx, n_gx), lax.rem(gy + s + n_gy, n_gy))

    def remote(src, dst, sems, slot, t, s):
        return pltpu.make_async_remote_copy(
            src_ref=src, dst_ref=dst, send_sem=sems.at[0, slot], recv_sem=sems.at[1, slot],
            device_id=peer(t, s), device_id_type=MESH)

    barrier = pltpu.get_barrier_semaphore()
    for t, s in PEERS:
        pl.semaphore_signal(barrier, inc=1, device_id=peer(-t, -s), device_id_type=MESH)
    loads = [pltpu.make_async_copy(h, v, in_sem.at[n]) for n, (h, v) in enumerate(
        ((cell_h, cell_v), (side_h, side_v), (frac_h, frac_v), (blade_h, blade_v), (dist_h, dist_v)))]
    for load in loads:
        load.start()
    for load in loads[:4]:
        load.wait()

    spots = lax.broadcasted_iota(jnp.int32, (2 * TY, MK), 0).astype(F32).astype(BF16)
    lines = lax.broadcasted_iota(jnp.int32, (CELLS, MK), 0).astype(F32).astype(BF16)
    one, zero = jnp.ones((), BF16), jnp.zeros((), BF16)

    def spread(x, j, n):
        return jnp.broadcast_to(x[j:j + 1, :], (n, MK))

    def place(b):
        cell = cell_v[pl.ds(b * 8, 8), :]
        spot = cell & (TY - 1)
        row = ((cell >> 7) & (TX - 1)) * NZ + (cell >> 9)
        return spot, row

    def halves(value):
        high = value.astype(BF16)
        return high, (value - high.astype(F32)).astype(BF16)

    def scatter_step(b, total):
        spot, row = place(b)
        spot = (spot + side_v[pl.ds(b * 8, 8), :] * TY).astype(F32).astype(BF16)
        row = row.astype(F32).astype(BF16)
        frac = frac_v[pl.ds(b * 8, 8), :]
        rest = 1.0 - frac
        pairs = []
        for c in range(3):
            blade = blade_v[c, pl.ds(b * 8, 8), :]
            pairs.append((halves(rest * blade), halves(frac * blade)))
        pairs.append((halves(rest * rest), halves(frac * frac)))
        pairs.append((halves(rest * frac), None))
        hot = jnp.concatenate([jnp.where(spots == spread(spot, j, 2 * TY), one, zero) for j in range(8)], axis=1)
        blocks = []
        for low, high in pairs:
            for h in range(2):
                parts = []
                for j in range(8):
                    line = spread(row, j, CELLS)
                    upper = zero if high is None else jnp.where(lines == line + 1, spread(high[h], j, CELLS), zero)
                    parts.append(jnp.where(lines == line, spread(low[h], j, CELLS), upper))
                blocks.append(jnp.concatenate(parts, axis=1))
        return total + lax.dot_general(jnp.concatenate(blocks, axis=0), hot, (((1,), (1,)), ((), ())),
                                       preferred_element_type=F32)

    total = lax.fori_loop(0, BL // 8, scatter_step, jnp.zeros((10 * CELLS, 2 * TY), F32), unroll=8)
    for n in range(5):
        both = total[2 * n * CELLS:(2 * n + 1) * CELLS] + total[(2 * n + 1) * CELLS:(2 * n + 2) * CELLS]
        g_v[n] = both[:, :TY]
        gf_v[n] = both[:, TY:]

    sides = ((ys_p, yr_p, yp_sem, YP, TY - 1, 1), (ys_n, yr_n, yn_sem, YN, 0, -1))
    fields = [[gf_v[n, rows(x), :] for x in range(TX)] for n in range(5)]
    for ref, _, _, _, column, _ in sides:
        ref[2:3, :] = packed(fields[:4], column)
        ref[3:4, :] = packed(fields[4:], column)
    pl.semaphore_wait(barrier, len(PEERS))
    send_y = []
    for ref, landing, sems, _, _, s in sides:
        send_y.append(remote(ref.at[2:4], landing.at[3, 2:4], sems, 3, 2, s))
    for copy in send_y:
        copy.start()

    loads[4].wait()
    for x in range(TX):
        values = [dist_v[i, planes(x), :] for i in range(19)]
        _, _, rho, jx, jy, jz = momentum_of(values)
        inv = 1.0 / rho
        for c, j in enumerate((jx, jy, jz)):
            vel_n[c, rows(x), :] = j * inv
        for i, post in enumerate(collided(values)):
            post_v[i, rows(x), :] = post

    for x in range(TX):
        own = force_of([g_v[n, rows(x), :] for n in range(5)], [vel_n[c, rows(x), :] for c in range(3)], 0)
        for i in range(1, 19):
            post_v[i, rows(x), :] = post_v[i, rows(x), :] + pushed(i, own)

    for ref, _, _, group, column, _ in sides:
        parts = ([[post_v[i, rows(x), :] for x in range(TX)] for i in group]
                 + [[vel_n[c, rows(x), :] for x in range(TX)] for c in range(3)])
        ref[0:1, :] = packed(parts[:4], column)
        ref[1:2, :] = packed(parts[4:], column)
    for ref, group, x in ((xs_p, XP, TX - 1), (xs_n, XN, 0)):
        for n, i in enumerate(group):
            ref[n] = post_v[i, rows(x), :]
    for c in range(3):
        xs_p[5 + c] = vel_n[c, rows(TX - 1), :]
        xs_n[5 + c] = vel_n[c, rows(0), :]

    later = []
    for n, t in ((2, 1), (1, 0), (0, -1)):
        part = slice(0, 2) if t == -1 else slice(0, 4)
        for ref, landing, sems, _, _, s in sides:
            later.append(remote(ref.at[part], landing.at[n, part], sems, n, t, s))
    send_vel = remote(vel_n, vel_f, v_sem, 0, -1, 0)
    send_x = [remote(gf_v, gr_1, g_sem, 0, 1, 0),
              remote(xs_p, xr_m, x_sem, 0, 1, 0),
              remote(gf_v.at[:, CELLS - NZ:, :], gr_2, g_sem, 1, 2, 0),
              remote(xs_n, xr_p, x_sem, 1, -1, 0)]
    for copy in later + [send_vel, send_x[1], send_x[3], send_x[2], send_x[0]]:
        copy.start()

    def interpolated(table, b):
        spot, row = place(b)
        frac = frac_v[pl.ds(b * 8, 8), :]
        rest = 1.0 - frac
        found = [jnp.zeros((8, MK), F32) for _ in range(3)]
        for r in range(CELLS):
            weight = jnp.where(row == r, rest, jnp.where(row == r - 1, frac, 0.0))
            for c in range(3):
                line = jnp.broadcast_to(table[c, r:r + 1, :], (8, TY))
                found[c] = found[c] + weight * jnp.take_along_axis(line, spot, axis=1)
        return found

    def near_step(b, carry):
        for c, found in enumerate(interpolated(vel_n, b)):
            mf_v[c, pl.ds(b * 8, 8), :] = STIFFNESS * (blade_v[c, pl.ds(b * 8, 8), :] - found)
        return carry

    def far_step(b, carry):
        far = side_v[pl.ds(b * 8, 8), :] == 1
        for c, found in enumerate(interpolated(vel_f, b)):
            force = STIFFNESS * (blade_v[c, pl.ds(b * 8, 8), :] - found)
            mf_v[c, pl.ds(b * 8, 8), :] = jnp.where(far, force, mf_v[c, pl.ds(b * 8, 8), :])
        return carry

    lax.fori_loop(0, BL // 8, near_step, 0, unroll=4)
    send_vel.wait()
    lax.fori_loop(0, BL // 8, far_step, 0, unroll=4)
    for copy in send_x:
        copy.wait()

    force = {}
    for x in range(-1, TX + 1):
        if x == -1:
            fields = [gr_2[n] for n in range(5)]
            vel = [xr_m[5 + c] for c in range(3)]
        elif x == TX:
            fields = [gf_v[n, rows(0), :] for n in range(5)]
            vel = [xr_p[5 + c] for c in range(3)]
        else:
            fields = [gr_1[n, rows(x), :] for n in range(5)]
            vel = [vel_n[c, rows(x), :] for c in range(3)]
        force[x] = force_of(fields, vel, 0)

    _, plane = lanes_and_planes()

    def post_at(i, x):
        if x == -1:
            value = xr_m[XP.index(i)]
        elif x == TX:
            value = xr_p[XN.index(i)]
        else:
            value = post_v[i, rows(x), :]
        push = pushed(i, force[x])
        return value if push is None else value + push

    def moved(i, x):
        value = post_at(i, x)
        cy = VELOCITIES[i][1]
        return value if cy == 0 else pltpu.roll(value, cy % TY, 1)

    for x in range(TX):
        for i in range(19):
            cx, _, cz = VELOCITIES[i]
            value = moved(i, x - cx)
            if cz == 1:
                value = jnp.where(plane == 0, post_at(opposite_of(i), x), pltpu.roll(value, 1, 0))
            elif cz == -1:
                value = jnp.where(plane == NZ - 1, moved(mirror_of(i), x - cx), pltpu.roll(value, NZ - 1, 0))
            new_v[i, planes(x), :] = value

    for copy in send_y + later:
        copy.wait_send()
    for copy in later + send_y:
        copy.wait_recv()


def finish(mid, mf, yr_p, yr_n, new_h, mf_h, new_v, sem):
    straight = [i for i in range(19) if VELOCITIES[i][1] == 0]
    copies = [pltpu.make_async_copy(mid.at[i], new_h.at[i], sem.at[i]) for i in straight]
    copies.append(pltpu.make_async_copy(mf, mf_h, sem.at[19]))
    for copy in copies:
        copy.start()
    lane, plane = lanes_and_planes()

    row = lax.broadcasted_iota(jnp.int32, (4, TY), 0)

    def source(first, second):
        return jnp.concatenate([jnp.where(row < 2, ref[first], ref[second]) for ref in (yr_p, yr_n)], axis=0)

    before, own, after = source(2, 3), source(1, 2), source(0, 1)
    lines = []
    for g in range(4):
        turn = TY - 4 * NZ * g
        line = jnp.where(lane < NZ, pltpu.roll(before, (turn - 3 * NZ) % TY, 1),
                         jnp.where(lane < 5 * NZ, pltpu.roll(own, (turn + NZ) % TY, 1),
                                   pltpu.roll(after, (turn + 5 * NZ) % TY, 1)))
        lines.append(jnp.where(lane < 6 * NZ, line, 0.0))
    edges = {}
    for n, group in enumerate((YP, YN)):
        line = [lines[q % 4][4 * n + q // 4:4 * n + q // 4 + 1, :] for q in range(13)]
        force = force_of(line[8:], line[5:8], 1)
        for q, i in enumerate(group):
            edges[i] = line[q] + pushed(i, force)

    def column(i, x):
        spot = lane == plane + (x + 1) * NZ
        return jnp.broadcast_to(
            jnp.sum(jnp.where(spot, jnp.broadcast_to(edges[i], (NZ, TY)), 0.0), axis=1, keepdims=True), (NZ, TY))

    for i in YP + YN:
        cx, cy, cz = VELOCITIES[i]
        here = lane == (0 if cy == 1 else TY - 1)
        for x in range(TX):
            value = column(i, x - cx)
            where = here
            if cz == 1:
                value = pltpu.roll(value, 1, 0)
                where = jnp.logical_and(here, plane > 0)
            elif cz == -1:
                value = jnp.where(plane == NZ - 1, column(mirror_of(i), x - cx), pltpu.roll(value, NZ - 1, 0))
            new_v[i, planes(x), :] = jnp.where(where, value, mid[i, planes(x), :])
        copy = pltpu.make_async_copy(new_v.at[i], new_h.at[i], sem.at[i])
        copy.start()
        copies.append(copy)
    for copy in copies:
        copy.wait()


def local(dist, marker_cell, marker_side, marker_frac, blade_vel):
    hbm = pl.BlockSpec(memory_space=pltpu.HBM)
    vmem = pl.BlockSpec(memory_space=pltpu.VMEM)
    cells = pltpu.VMEM((19, CELLS, TY), F32)
    field = pltpu.VMEM((3, CELLS, TY), F32)
    edge = pltpu.VMEM((4, TY), F32)
    dma = pltpu.SemaphoreType.DMA
    shape = jax.ShapeDtypeStruct
    given = [pltpu.with_memory_space_constraint(a, pltpu.HBM) for a in (
        dist.reshape(19, CELLS, TY), marker_cell, marker_side, marker_frac, blade_vel)]
    mid, mf, yr_p, yr_n = pl.pallas_call(
        exchange,
        out_shape=(shape((19, CELLS, TY), F32), shape((3, BL, MK), F32),
                   shape((4, 4, TY), F32), shape((4, 4, TY), F32)),
        in_specs=[hbm] * 5,
        out_specs=(vmem,) * 4,
        scratch_shapes=[
            cells, pltpu.VMEM((BL, MK), jnp.int32), pltpu.VMEM((BL, MK), jnp.int32), pltpu.VMEM((BL, MK), F32),
            pltpu.VMEM((3, BL, MK), F32),
            field, field, cells, pltpu.VMEM((8, NZ, TY), F32), pltpu.VMEM((8, NZ, TY), F32),
            pltpu.VMEM((8, NZ, TY), F32), pltpu.VMEM((8, NZ, TY), F32),
            pltpu.VMEM((5, CELLS, TY), F32), pltpu.VMEM((5, CELLS, TY), F32), pltpu.VMEM((5, CELLS, TY), F32), pltpu.VMEM((5, NZ, TY), F32),
            edge, edge,
            dma((5,)), dma((2, 1)), dma((2, 2)), dma((2, 2)), dma((2, 4)), dma((2, 4)),
        ],
        compiler_params=pltpu.CompilerParams(collective_id=0, has_side_effects=True, vmem_limit_bytes=32 * 2**20),
        name="exchange",
    )(*given)
    new, force = pl.pallas_call(
        finish,
        out_shape=(shape((19, CELLS, TY), F32), shape((3, BL, MK), F32)),
        in_specs=[vmem] * 4,
        out_specs=(hbm, hbm),
        scratch_shapes=[cells, dma((20,))],
        compiler_params=pltpu.CompilerParams(vmem_limit_bytes=16 * 2**20),
        name="finish",
    )(mid, mf, yr_p, yr_n)
    return new.reshape(dist.shape), force


def solution(mesh):
    return jax.shard_map(
        local,
        mesh=mesh,
        in_specs=(
            P(None, None, "gx", "gy"),
            P(("gx", "gy"), None),
            P(("gx", "gy"), None),
            P(("gx", "gy"), None),
            P(None, ("gx", "gy"), None),
        ),
        out_specs=(P(None, None, "gx", "gy"), P(None, ("gx", "gy"), None)),
        check_vma=False,
    )
```

```python
import jax
import jax.numpy as jnp
from jax import lax
from jax.experimental import pallas as pl
from jax.experimental.pallas import tpu as pltpu
from jax.sharding import PartitionSpec as P

VELOCITIES = [
    (0, 0, 0), (1, 0, 0), (-1, 0, 0), (0, 1, 0), (0, -1, 0), (0, 0, 1), (0, 0, -1),
    (1, 1, 0), (-1, -1, 0), (1, -1, 0), (-1, 1, 0), (1, 0, 1), (-1, 0, -1), (1, 0, -1),
    (-1, 0, 1), (0, 1, 1), (0, -1, -1), (0, 1, -1), (0, -1, 1),
]
WEIGHTS = [1.0 / 3.0] + [1.0 / 18.0] * 6 + [1.0 / 36.0] * 12
RATE2, RATE3, RATE4 = 1.6, 1.2, 1.4
STIFFNESS = 2.0

NZ, TX, TY = 8, 4, 128
BL, MK = 64, 128
CELLS = TX * NZ
F32, BF16 = jnp.float32, jnp.bfloat16
MESH = pl.DeviceIdType.MESH

XP = [i for i in range(19) if VELOCITIES[i][0] == 1]
XN = [i for i in range(19) if VELOCITIES[i][0] == -1]
YP = [i for i in range(19) if VELOCITIES[i][1] == 1]
YN = [i for i in range(19) if VELOCITIES[i][1] == -1]
HOPS = (-1, 0, 1, 2)
PEERS = [(t, s) for t in HOPS for s in (-1, 0, 1) if (t, s) != (0, 0)]


def opposite_of(i):
    return VELOCITIES.index(tuple(-c for c in VELOCITIES[i]))


def mirror_of(i):
    a, b, c = VELOCITIES[i]
    return VELOCITIES.index((a, b, -c))


def momentum_of(f):
    s = [f[2 * p + 1] + f[2 * p + 2] for p in range(9)]
    d = [f[2 * p + 1] - f[2 * p + 2] for p in range(9)]
    pxy, pxz, pyz = s[3] + s[4], s[5] + s[6], s[7] + s[8]
    density = f[0] + s[0] + s[1] + s[2] + pxy + pxz + pyz
    jx = d[0] + (d[3] + d[4]) + (d[5] + d[6])
    jy = d[1] + (d[3] - d[4]) + (d[7] + d[8])
    jz = d[2] + (d[5] - d[6]) + (d[7] - d[8])
    return s, d, density, jx, jy, jz


def collided(f):
    s, d, rho, jx, jy, jz = momentum_of(f)
    inv = 1.0 / rho
    ux, uy, uz = jx * inv, jy * inv, jz * inv
    ax, ay, az = jx * ux, jy * uy, jz * uz
    third, ninth = rho * (1.0 / 3.0), rho * (1.0 / 9.0)
    sixth = (ax + ay + az) * (1.0 / 6.0)
    pxy, pxz, pyz = s[3] + s[4], s[5] + s[6], s[7] + s[8]
    nxx = RATE2 * (s[0] + pxy + pxz - third - ax)
    nyy = RATE2 * (s[1] + pxy + pyz - third - ay)
    nzz = RATE2 * (s[2] + pxz + pyz - third - az)
    nxy = RATE2 * (s[3] - s[4] - jx * uy)
    nxz = RATE2 * (s[5] - s[6] - jx * uz)
    nyz = RATE2 * (s[7] - s[8] - jy * uz)
    tx, ty, tz = jx * (1.0 / 3.0), jy * (1.0 / 3.0), jz * (1.0 / 3.0)
    nxxy = RATE3 * (d[3] - d[4] - ty)
    nxyy = RATE3 * (d[3] + d[4] - tx)
    nxxz = RATE3 * (d[5] - d[6] - tz)
    nxzz = RATE3 * (d[5] + d[6] - tx)
    nyyz = RATE3 * (d[7] - d[8] - tz)
    nyzz = RATE3 * (d[7] + d[8] - ty)
    base = ninth - sixth
    qxy = RATE4 * (pxy - base - 0.5 * (ax + ay))
    qxz = RATE4 * (pxz - base - 0.5 * (ax + az))
    qyz = RATE4 * (pyz - base - 0.5 * (ay + az))
    even = [
        0.5 * (nxx - qxy - qxz), 0.5 * (nyy - qxy - qyz), 0.5 * (nzz - qxz - qyz),
        0.25 * (qxy + nxy), 0.25 * (qxy - nxy),
        0.25 * (qxz + nxz), 0.25 * (qxz - nxz),
        0.25 * (qyz + nyz), 0.25 * (qyz - nyz),
    ]
    odd = [
        -0.5 * (nxyy + nxzz), -0.5 * (nxxy + nyzz), -0.5 * (nxxz + nyyz),
        0.25 * (nxyy + nxxy), 0.25 * (nxyy - nxxy),
        0.25 * (nxzz + nxxz), 0.25 * (nxzz - nxxz),
        0.25 * (nyzz + nyyz), 0.25 * (nyzz - nyyz),
    ]
    out = [f[0] + (nxx + nyy + nzz - qxy - qxz - qyz)]
    for p in range(9):
        out.append(f[2 * p + 1] - (even[p] + odd[p]))
        out.append(f[2 * p + 2] - (even[p] - odd[p]))
    return out


def pushed(i, force):
    total = None
    for c, part in zip(VELOCITIES[i], force):
        if c != 0:
            term = part if c > 0 else -part
            total = term if total is None else total + term
    return None if total is None else (3.0 * WEIGHTS[i]) * total


def rows(x):
    return pl.ds(x * NZ, NZ)


def planes(x):
    return pl.ds(x, NZ, stride=TX)


def lanes_and_planes():
    return (lax.broadcasted_iota(jnp.int32, (NZ, TY), 1), lax.broadcasted_iota(jnp.int32, (NZ, TY), 0))


def packed(groups, column):
    lane, plane = lanes_and_planes()
    total = None
    for g, blocks in enumerate(groups):
        for n, block in enumerate(blocks):
            part = jnp.where(lane == plane + (g * TX + n) * NZ,
                             jnp.broadcast_to(block[:, column:column + 1], (NZ, TY)), 0.0)
            total = part if total is None else total + part
    return jnp.sum(total, axis=0, keepdims=True)


def force_of(fields, vel, axis):
    size = vel[0].shape[axis]
    out = []
    for c in range(3):
        below = pltpu.roll(fields[4] * vel[c], 1, axis)
        above = fields[4] * pltpu.roll(vel[c], size - 1, axis)
        out.append(STIFFNESS * (fields[c] - fields[3] * vel[c] - above - below))
    return out


def exchange(dist_h, cell_h, side_h, frac_h, blade_h, new_v, mf_v, yr_p, yr_n,
             dist_v, cell_v, side_v, frac_v, blade_v,
             vel_n, vel_f, post_v, xs_p, xs_n, xr_m, xr_p,
             g_v, gf_v, gr_1, gr_2, ys_p, ys_n,
             in_sem, v_sem, x_sem, g_sem, yp_sem, yn_sem):
    n_gx, n_gy = lax.axis_size("gx"), lax.axis_size("gy")
    gx, gy = lax.axis_index("gx"), lax.axis_index("gy")

    def peer(t, s):
        return (lax.rem(gx + t + n_gx, n_gx), lax.rem(gy + s + n_gy, n_gy))

    def remote(src, dst, sems, slot, t, s):
        return pltpu.make_async_remote_copy(
            src_ref=src, dst_ref=dst, send_sem=sems.at[0, slot], recv_sem=sems.at[1, slot],
            device_id=peer(t, s), device_id_type=MESH)

    barrier = pltpu.get_barrier_semaphore()
    for t, s in PEERS:
        pl.semaphore_signal(barrier, inc=1, device_id=peer(-t, -s), device_id_type=MESH)
    loads = [pltpu.make_async_copy(h, v, in_sem.at[n]) for n, (h, v) in enumerate(
        ((cell_h, cell_v), (side_h, side_v), (frac_h, frac_v), (blade_h, blade_v), (dist_h, dist_v)))]
    for load in loads:
        load.start()
    for load in loads[:4]:
        load.wait()

    spots = lax.broadcasted_iota(jnp.int32, (2 * TY, MK), 0).astype(F32).astype(BF16)
    lines = lax.broadcasted_iota(jnp.int32, (CELLS, MK), 0).astype(F32).astype(BF16)
    one, zero = jnp.ones((), BF16), jnp.zeros((), BF16)

    def spread(x, j, n):
        return jnp.broadcast_to(x[j:j + 1, :], (n, MK))

    def place(b):
        cell = cell_v[pl.ds(b * 8, 8), :]
        spot = cell & (TY - 1)
        row = ((cell >> 7) & (TX - 1)) * NZ + (cell >> 9)
        return spot, row

    def halves(value):
        high = value.astype(BF16)
        return high, (value - high.astype(F32)).astype(BF16)

    def scatter_step(b, total):
        spot, row = place(b)
        spot = (spot + side_v[pl.ds(b * 8, 8), :] * TY).astype(F32).astype(BF16)
        row = row.astype(F32).astype(BF16)
        frac = frac_v[pl.ds(b * 8, 8), :]
        rest = 1.0 - frac
        pairs = []
        for c in range(3):
            blade = blade_v[c, pl.ds(b * 8, 8), :]
            pairs.append((halves(rest * blade), halves(frac * blade)))
        pairs.append((halves(rest * rest), halves(frac * frac)))
        pairs.append((halves(rest * frac), None))
        hot = jnp.concatenate([jnp.where(spots == spread(spot, j, 2 * TY), one, zero) for j in range(8)], axis=1)
        blocks = []
        for low, high in pairs:
            for h in range(2):
                parts = []
                for j in range(8):
                    line = spread(row, j, CELLS)
                    upper = zero if high is None else jnp.where(lines == line + 1, spread(high[h], j, CELLS), zero)
                    parts.append(jnp.where(lines == line, spread(low[h], j, CELLS), upper))
                blocks.append(jnp.concatenate(parts, axis=1))
        return total + lax.dot_general(jnp.concatenate(blocks, axis=0), hot, (((1,), (1,)), ((), ())),
                                       preferred_element_type=F32)

    total = lax.fori_loop(0, BL // 8, scatter_step, jnp.zeros((10 * CELLS, 2 * TY), F32), unroll=8)
    for n in range(5):
        both = total[2 * n * CELLS:(2 * n + 1) * CELLS] + total[(2 * n + 1) * CELLS:(2 * n + 2) * CELLS]
        g_v[n] = both[:, :TY]
        gf_v[n] = both[:, TY:]

    sides = ((ys_p, yr_p, yp_sem, YP, TY - 1, 1), (ys_n, yr_n, yn_sem, YN, 0, -1))
    fields = [[gf_v[n, rows(x), :] for x in range(TX)] for n in range(5)]
    for ref, _, _, _, column, _ in sides:
        ref[2:3, :] = packed(fields[:4], column)
        ref[3:4, :] = packed(fields[4:], column)
    pl.semaphore_wait(barrier, len(PEERS))
    send_y = []
    for ref, landing, sems, _, _, s in sides:
        send_y.append(remote(ref.at[2:4], landing.at[3, 2:4], sems, 3, 2, s))
    for copy in send_y:
        copy.start()

    loads[4].wait()
    for x in range(TX):
        values = [dist_v[i, planes(x), :] for i in range(19)]
        _, _, rho, jx, jy, jz = momentum_of(values)
        inv = 1.0 / rho
        for c, j in enumerate((jx, jy, jz)):
            vel_n[c, rows(x), :] = j * inv
        for i, post in enumerate(collided(values)):
            post_v[i, rows(x), :] = post

    for x in range(TX):
        own = force_of([g_v[n, rows(x), :] for n in range(5)], [vel_n[c, rows(x), :] for c in range(3)], 0)
        for i in range(1, 19):
            post_v[i, rows(x), :] = post_v[i, rows(x), :] + pushed(i, own)

    for ref, _, _, group, column, _ in sides:
        parts = ([[post_v[i, rows(x), :] for x in range(TX)] for i in group]
                 + [[vel_n[c, rows(x), :] for x in range(TX)] for c in range(3)])
        ref[0:1, :] = packed(parts[:4], column)
        ref[1:2, :] = packed(parts[4:], column)
    for ref, group, x in ((xs_p, XP, TX - 1), (xs_n, XN, 0)):
        for n, i in enumerate(group):
            ref[n] = post_v[i, rows(x), :]
    for c in range(3):
        xs_p[5 + c] = vel_n[c, rows(TX - 1), :]
        xs_n[5 + c] = vel_n[c, rows(0), :]

    later = []
    for n, t in ((2, 1), (1, 0), (0, -1)):
        part = slice(0, 2) if t == -1 else slice(0, 4)
        for ref, landing, sems, _, _, s in sides:
            later.append(remote(ref.at[part], landing.at[n, part], sems, n, t, s))
    send_vel = remote(vel_n, vel_f, v_sem, 0, -1, 0)
    send_x = [remote(gf_v, gr_1, g_sem, 0, 1, 0),
              remote(xs_p, xr_m, x_sem, 0, 1, 0),
              remote(gf_v.at[:, CELLS - NZ:, :], gr_2, g_sem, 1, 2, 0),
              remote(xs_n, xr_p, x_sem, 1, -1, 0)]
    for copy in later + [send_vel, send_x[1], send_x[3], send_x[2], send_x[0]]:
        copy.start()

    def interpolated(table, b):
        spot, row = place(b)
        frac = frac_v[pl.ds(b * 8, 8), :]
        rest = 1.0 - frac
        found = [jnp.zeros((8, MK), F32) for _ in range(3)]
        for r in range(CELLS):
            weight = jnp.where(row == r, rest, jnp.where(row == r - 1, frac, 0.0))
            for c in range(3):
                line = jnp.broadcast_to(table[c, r:r + 1, :], (8, TY))
                found[c] = found[c] + weight * jnp.take_along_axis(line, spot, axis=1)
        return found

    def near_step(b, carry):
        for c, found in enumerate(interpolated(vel_n, b)):
            mf_v[c, pl.ds(b * 8, 8), :] = STIFFNESS * (blade_v[c, pl.ds(b * 8, 8), :] - found)
        return carry

    def far_step(b, carry):
        far = side_v[pl.ds(b * 8, 8), :] == 1
        for c, found in enumerate(interpolated(vel_f, b)):
            force = STIFFNESS * (blade_v[c, pl.ds(b * 8, 8), :] - found)
            mf_v[c, pl.ds(b * 8, 8), :] = jnp.where(far, force, mf_v[c, pl.ds(b * 8, 8), :])
        return carry

    lax.fori_loop(0, BL // 8, near_step, 0, unroll=4)
    send_vel.wait()
    lax.fori_loop(0, BL // 8, far_step, 0, unroll=4)
    for copy in send_x:
        copy.wait()

    force = {}
    for x in range(-1, TX + 1):
        if x == -1:
            fields = [gr_2[n] for n in range(5)]
            vel = [xr_m[5 + c] for c in range(3)]
        elif x == TX:
            fields = [gf_v[n, rows(0), :] for n in range(5)]
            vel = [xr_p[5 + c] for c in range(3)]
        else:
            fields = [gr_1[n, rows(x), :] for n in range(5)]
            vel = [vel_n[c, rows(x), :] for c in range(3)]
        force[x] = force_of(fields, vel, 0)

    _, plane = lanes_and_planes()

    def post_at(i, x):
        if x == -1:
            value = xr_m[XP.index(i)]
        elif x == TX:
            value = xr_p[XN.index(i)]
        else:
            value = post_v[i, rows(x), :]
        push = pushed(i, force[x])
        return value if push is None else value + push

    def moved(i, x):
        value = post_at(i, x)
        cy = VELOCITIES[i][1]
        return value if cy == 0 else pltpu.roll(value, cy % TY, 1)

    for x in range(TX):
        for i in range(19):
            cx, _, cz = VELOCITIES[i]
            value = moved(i, x - cx)
            if cz == 1:
                value = jnp.where(plane == 0, post_at(opposite_of(i), x), pltpu.roll(value, 1, 0))
            elif cz == -1:
                value = jnp.where(plane == NZ - 1, moved(mirror_of(i), x - cx), pltpu.roll(value, NZ - 1, 0))
            new_v[i, planes(x), :] = value

    for copy in send_y + later:
        copy.wait_send()
    for copy in later + send_y:
        copy.wait_recv()


def finish(mid, mf, yr_p, yr_n, new_v, mf_v):
    for i in range(19):
        if VELOCITIES[i][1] == 0:
            new_v[i] = mid[i]
    mf_v[...] = mf[...]
    lane, plane = lanes_and_planes()

    row = lax.broadcasted_iota(jnp.int32, (4, TY), 0)

    def source(first, second):
        return jnp.concatenate([jnp.where(row < 2, ref[first], ref[second]) for ref in (yr_p, yr_n)], axis=0)

    before, own, after = source(2, 3), source(1, 2), source(0, 1)
    lines = []
    for g in range(4):
        turn = TY - 4 * NZ * g
        line = jnp.where(lane < NZ, pltpu.roll(before, (turn - 3 * NZ) % TY, 1),
                         jnp.where(lane < 5 * NZ, pltpu.roll(own, (turn + NZ) % TY, 1),
                                   pltpu.roll(after, (turn + 5 * NZ) % TY, 1)))
        lines.append(jnp.where(lane < 6 * NZ, line, 0.0))
    edges = {}
    for n, group in enumerate((YP, YN)):
        line = [lines[q % 4][4 * n + q // 4:4 * n + q // 4 + 1, :] for q in range(13)]
        force = force_of(line[8:], line[5:8], 1)
        for q, i in enumerate(group):
            edges[i] = line[q] + pushed(i, force)

    columns = {}

    def column(i, x):
        if (i, x) not in columns:
            spot = lane == plane + (x + 1) * NZ
            column = jnp.sum(jnp.where(spot, jnp.broadcast_to(edges[i], (NZ, TY)), 0.0), axis=1, keepdims=True)
            columns[i, x] = jnp.broadcast_to(column, (NZ, TY))
        return columns[i, x]

    for i in YP + YN:
        cx, cy, cz = VELOCITIES[i]
        here = lane == (0 if cy == 1 else TY - 1)
        for x in range(TX):
            value = column(i, x - cx)
            where = here
            if cz == 1:
                value = pltpu.roll(value, 1, 0)
                where = jnp.logical_and(here, plane > 0)
            elif cz == -1:
                value = jnp.where(plane == NZ - 1, column(mirror_of(i), x - cx), pltpu.roll(value, NZ - 1, 0))
            new_v[i, planes(x), :] = jnp.where(where, value, mid[i, planes(x), :])


def local(dist, marker_cell, marker_side, marker_frac, blade_vel):
    hbm = pl.BlockSpec(memory_space=pltpu.HBM)
    vmem = pl.BlockSpec(memory_space=pltpu.VMEM)
    cells = pltpu.VMEM((19, CELLS, TY), F32)
    field = pltpu.VMEM((3, CELLS, TY), F32)
    edge = pltpu.VMEM((4, TY), F32)
    dma = pltpu.SemaphoreType.DMA
    shape = jax.ShapeDtypeStruct
    given = [pltpu.with_memory_space_constraint(a, pltpu.HBM) for a in (
        dist.reshape(19, CELLS, TY), marker_cell, marker_side, marker_frac, blade_vel)]
    mid, mf, yr_p, yr_n = pl.pallas_call(
        exchange,
        out_shape=(shape((19, CELLS, TY), F32), shape((3, BL, MK), F32),
                   shape((4, 4, TY), F32), shape((4, 4, TY), F32)),
        in_specs=[hbm] * 5,
        out_specs=(vmem,) * 4,
        scratch_shapes=[
            cells, pltpu.VMEM((BL, MK), jnp.int32), pltpu.VMEM((BL, MK), jnp.int32), pltpu.VMEM((BL, MK), F32),
            pltpu.VMEM((3, BL, MK), F32),
            field, field, cells, pltpu.VMEM((8, NZ, TY), F32), pltpu.VMEM((8, NZ, TY), F32),
            pltpu.VMEM((8, NZ, TY), F32), pltpu.VMEM((8, NZ, TY), F32),
            pltpu.VMEM((5, CELLS, TY), F32), pltpu.VMEM((5, CELLS, TY), F32), pltpu.VMEM((5, CELLS, TY), F32), pltpu.VMEM((5, NZ, TY), F32),
            edge, edge,
            dma((5,)), dma((2, 1)), dma((2, 2)), dma((2, 2)), dma((2, 4)), dma((2, 4)),
        ],
        compiler_params=pltpu.CompilerParams(collective_id=0, has_side_effects=True, vmem_limit_bytes=32 * 2**20),
        name="exchange",
    )(*given)
    new, force = pl.pallas_call(
        finish,
        out_shape=(shape((19, CELLS, TY), F32), shape((3, BL, MK), F32)),
        in_specs=[vmem] * 4,
        out_specs=(vmem, vmem),
        compiler_params=pltpu.CompilerParams(vmem_limit_bytes=16 * 2**20),
        name="finish",
    )(mid, mf, yr_p, yr_n)
    return new.reshape(dist.shape), force


def solution(mesh):
    return jax.shard_map(
        local,
        mesh=mesh,
        in_specs=(
            P(None, None, "gx", "gy"),
            P(("gx", "gy"), None),
            P(("gx", "gy"), None),
            P(("gx", "gy"), None),
            P(None, ("gx", "gy"), None),
        ),
        out_specs=(P(None, None, "gx", "gy"), P(None, ("gx", "gy"), None)),
        check_vma=False,
    )
```

```python
import jax
import jax.numpy as jnp
from jax import lax
from jax.experimental import pallas as pl
from jax.experimental.pallas import tpu as pltpu
from jax.sharding import PartitionSpec as P

VELOCITIES = [
    (0, 0, 0), (1, 0, 0), (-1, 0, 0), (0, 1, 0), (0, -1, 0), (0, 0, 1), (0, 0, -1),
    (1, 1, 0), (-1, -1, 0), (1, -1, 0), (-1, 1, 0), (1, 0, 1), (-1, 0, -1), (1, 0, -1),
    (-1, 0, 1), (0, 1, 1), (0, -1, -1), (0, 1, -1), (0, -1, 1),
]
WEIGHTS = [1.0 / 3.0] + [1.0 / 18.0] * 6 + [1.0 / 36.0] * 12
RATE2, RATE3, RATE4 = 1.6, 1.2, 1.4
STIFFNESS = 2.0

NZ, TX, TY = 8, 4, 128
BL, MK = 64, 128
CELLS = TX * NZ
F32, BF16 = jnp.float32, jnp.bfloat16
MESH = pl.DeviceIdType.MESH

XP = [i for i in range(19) if VELOCITIES[i][0] == 1]
XN = [i for i in range(19) if VELOCITIES[i][0] == -1]
YP = [i for i in range(19) if VELOCITIES[i][1] == 1]
YN = [i for i in range(19) if VELOCITIES[i][1] == -1]
HOPS = (-1, 0, 1, 2)
PEERS = [(t, s) for t in HOPS for s in (-1, 0, 1) if (t, s) != (0, 0)]


def opposite_of(i):
    return VELOCITIES.index(tuple(-c for c in VELOCITIES[i]))


def mirror_of(i):
    a, b, c = VELOCITIES[i]
    return VELOCITIES.index((a, b, -c))


def momentum_of(f):
    s = [f[2 * p + 1] + f[2 * p + 2] for p in range(9)]
    d = [f[2 * p + 1] - f[2 * p + 2] for p in range(9)]
    pxy, pxz, pyz = s[3] + s[4], s[5] + s[6], s[7] + s[8]
    density = f[0] + s[0] + s[1] + s[2] + pxy + pxz + pyz
    jx = d[0] + (d[3] + d[4]) + (d[5] + d[6])
    jy = d[1] + (d[3] - d[4]) + (d[7] + d[8])
    jz = d[2] + (d[5] - d[6]) + (d[7] - d[8])
    return s, d, density, jx, jy, jz


def collided(f):
    s, d, rho, jx, jy, jz = momentum_of(f)
    inv = 1.0 / rho
    ux, uy, uz = jx * inv, jy * inv, jz * inv
    ax, ay, az = jx * ux, jy * uy, jz * uz
    third, ninth = rho * (1.0 / 3.0), rho * (1.0 / 9.0)
    sixth = (ax + ay + az) * (1.0 / 6.0)
    pxy, pxz, pyz = s[3] + s[4], s[5] + s[6], s[7] + s[8]
    nxx = RATE2 * (s[0] + pxy + pxz - third - ax)
    nyy = RATE2 * (s[1] + pxy + pyz - third - ay)
    nzz = RATE2 * (s[2] + pxz + pyz - third - az)
    nxy = RATE2 * (s[3] - s[4] - jx * uy)
    nxz = RATE2 * (s[5] - s[6] - jx * uz)
    nyz = RATE2 * (s[7] - s[8] - jy * uz)
    tx, ty, tz = jx * (1.0 / 3.0), jy * (1.0 / 3.0), jz * (1.0 / 3.0)
    nxxy = RATE3 * (d[3] - d[4] - ty)
    nxyy = RATE3 * (d[3] + d[4] - tx)
    nxxz = RATE3 * (d[5] - d[6] - tz)
    nxzz = RATE3 * (d[5] + d[6] - tx)
    nyyz = RATE3 * (d[7] - d[8] - tz)
    nyzz = RATE3 * (d[7] + d[8] - ty)
    base = ninth - sixth
    qxy = RATE4 * (pxy - base - 0.5 * (ax + ay))
    qxz = RATE4 * (pxz - base - 0.5 * (ax + az))
    qyz = RATE4 * (pyz - base - 0.5 * (ay + az))
    even = [
        0.5 * (nxx - qxy - qxz), 0.5 * (nyy - qxy - qyz), 0.5 * (nzz - qxz - qyz),
        0.25 * (qxy + nxy), 0.25 * (qxy - nxy),
        0.25 * (qxz + nxz), 0.25 * (qxz - nxz),
        0.25 * (qyz + nyz), 0.25 * (qyz - nyz),
    ]
    odd = [
        -0.5 * (nxyy + nxzz), -0.5 * (nxxy + nyzz), -0.5 * (nxxz + nyyz),
        0.25 * (nxyy + nxxy), 0.25 * (nxyy - nxxy),
        0.25 * (nxzz + nxxz), 0.25 * (nxzz - nxxz),
        0.25 * (nyzz + nyyz), 0.25 * (nyzz - nyyz),
    ]
    out = [f[0] + (nxx + nyy + nzz - qxy - qxz - qyz)]
    for p in range(9):
        out.append(f[2 * p + 1] - (even[p] + odd[p]))
        out.append(f[2 * p + 2] - (even[p] - odd[p]))
    return out


def pushed(i, force):
    total = None
    for c, part in zip(VELOCITIES[i], force):
        if c != 0:
            term = part if c > 0 else -part
            total = term if total is None else total + term
    return None if total is None else (3.0 * WEIGHTS[i]) * total


def rows(x):
    return pl.ds(x * NZ, NZ)


def planes(x):
    return pl.ds(x, NZ, stride=TX)


def lanes_and_planes():
    return (lax.broadcasted_iota(jnp.int32, (NZ, TY), 1), lax.broadcasted_iota(jnp.int32, (NZ, TY), 0))


def packed(groups, column):
    lane, plane = lanes_and_planes()
    total = None
    for g, blocks in enumerate(groups):
        for n, block in enumerate(blocks):
            part = jnp.where(lane == plane + (g * TX + n) * NZ,
                             jnp.broadcast_to(block[:, column:column + 1], (NZ, TY)), 0.0)
            total = part if total is None else total + part
    return jnp.sum(total, axis=0, keepdims=True)


def force_of(fields, vel, axis):
    size = vel[0].shape[axis]
    out = []
    for c in range(3):
        below = pltpu.roll(fields[4] * vel[c], 1, axis)
        above = fields[4] * pltpu.roll(vel[c], size - 1, axis)
        out.append(STIFFNESS * (fields[c] - fields[3] * vel[c] - above - below))
    return out


def exchange(dist_h, cell_h, side_h, frac_h, blade_h, new_v, mf_v, yr_p, yr_n,
             dist_v, cell_v, side_v, frac_v, blade_v,
             vel_n, vel_f, post_v, xs_p, xs_n, xr_m, xr_p,
             g_v, gf_v, gr_1, gr_2, ys_p, ys_n,
             in_sem, v_sem, x_sem, g_sem, yp_sem, yn_sem):
    n_gx, n_gy = lax.axis_size("gx"), lax.axis_size("gy")
    gx, gy = lax.axis_index("gx"), lax.axis_index("gy")

    def peer(t, s):
        return (lax.rem(gx + t + n_gx, n_gx), lax.rem(gy + s + n_gy, n_gy))

    def remote(src, dst, sems, slot, t, s):
        return pltpu.make_async_remote_copy(
            src_ref=src, dst_ref=dst, send_sem=sems.at[0, slot], recv_sem=sems.at[1, slot],
            device_id=peer(t, s), device_id_type=MESH)

    barrier = pltpu.get_barrier_semaphore()
    for t, s in PEERS:
        pl.semaphore_signal(barrier, inc=1, device_id=peer(-t, -s), device_id_type=MESH)
    loads = [pltpu.make_async_copy(h, v, in_sem.at[n]) for n, (h, v) in enumerate(
        ((cell_h, cell_v), (side_h, side_v), (frac_h, frac_v), (blade_h, blade_v), (dist_h, dist_v)))]
    for load in loads:
        load.start()
    for load in loads[:4]:
        load.wait()

    spots = lax.broadcasted_iota(jnp.int32, (2 * TY, MK), 0).astype(F32).astype(BF16)
    lines = lax.broadcasted_iota(jnp.int32, (CELLS, MK), 0).astype(F32).astype(BF16)
    one, zero = jnp.ones((), BF16), jnp.zeros((), BF16)

    def spread(x, j, n):
        return jnp.broadcast_to(x[j:j + 1, :], (n, MK))

    def place(b):
        cell = cell_v[pl.ds(b * 8, 8), :]
        spot = cell & (TY - 1)
        row = ((cell >> 7) & (TX - 1)) * NZ + (cell >> 9)
        return spot, row

    def halves(value):
        high = value.astype(BF16)
        return high, (value - high.astype(F32)).astype(BF16)

    def scatter_step(b, total):
        spot, row = place(b)
        spot = (spot + side_v[pl.ds(b * 8, 8), :] * TY).astype(F32).astype(BF16)
        row = row.astype(F32).astype(BF16)
        frac = frac_v[pl.ds(b * 8, 8), :]
        rest = 1.0 - frac
        pairs = []
        for c in range(3):
            blade = blade_v[c, pl.ds(b * 8, 8), :]
            pairs.append((halves(rest * blade), halves(frac * blade)))
        pairs.append((halves(rest * rest), halves(frac * frac)))
        pairs.append((halves(rest * frac), None))
        hot = jnp.concatenate([jnp.where(spots == spread(spot, j, 2 * TY), one, zero) for j in range(8)], axis=1)
        blocks = []
        for low, high in pairs:
            for h in range(2):
                parts = []
                for j in range(8):
                    line = spread(row, j, CELLS)
                    upper = zero if high is None else jnp.where(lines == line + 1, spread(high[h], j, CELLS), zero)
                    parts.append(jnp.where(lines == line, spread(low[h], j, CELLS), upper))
                blocks.append(jnp.concatenate(parts, axis=1))
        return total + lax.dot_general(jnp.concatenate(blocks, axis=0), hot, (((1,), (1,)), ((), ())),
                                       preferred_element_type=F32)

    total = lax.fori_loop(0, BL // 8, scatter_step, jnp.zeros((10 * CELLS, 2 * TY), F32), unroll=8)
    for n in range(5):
        both = total[2 * n * CELLS:(2 * n + 1) * CELLS] + total[(2 * n + 1) * CELLS:(2 * n + 2) * CELLS]
        g_v[n] = both[:, :TY]
        gf_v[n] = both[:, TY:]

    sides = ((ys_p, yr_p, yp_sem, YP, TY - 1, 1), (ys_n, yr_n, yn_sem, YN, 0, -1))
    fields = [[gf_v[n, rows(x), :] for x in range(TX)] for n in range(5)]
    for ref, _, _, _, column, _ in sides:
        ref[2:3, :] = packed(fields[:4], column)
        ref[3:4, :] = packed(fields[4:], column)
    pl.semaphore_wait(barrier, len(PEERS))
    send_y = []
    for ref, landing, sems, _, _, s in sides:
        send_y.append(remote(ref.at[2:4], landing.at[3, 2:4], sems, 3, 2, s))
    for copy in send_y:
        copy.start()

    loads[4].wait()
    for x in range(TX):
        values = [dist_v[i, planes(x), :] for i in range(19)]
        _, _, rho, jx, jy, jz = momentum_of(values)
        inv = 1.0 / rho
        for c, j in enumerate((jx, jy, jz)):
            vel_n[c, rows(x), :] = j * inv
        for i, post in enumerate(collided(values)):
            post_v[i, rows(x), :] = post

    for x in range(TX):
        own = force_of([g_v[n, rows(x), :] for n in range(5)], [vel_n[c, rows(x), :] for c in range(3)], 0)
        for i in range(1, 19):
            post_v[i, rows(x), :] = post_v[i, rows(x), :] + pushed(i, own)

    for ref, _, _, group, column, _ in sides:
        parts = ([[post_v[i, rows(x), :] for x in range(TX)] for i in group]
                 + [[vel_n[c, rows(x), :] for x in range(TX)] for c in range(3)])
        ref[0:1, :] = packed(parts[:4], column)
        ref[1:2, :] = packed(parts[4:], column)
    for ref, group, x in ((xs_p, XP, TX - 1), (xs_n, XN, 0)):
        for n, i in enumerate(group):
            ref[n] = post_v[i, rows(x), :]
    for c in range(3):
        xs_p[5 + c] = vel_n[c, rows(TX - 1), :]
        xs_n[5 + c] = vel_n[c, rows(0), :]

    later = []
    for n, t in ((0, -1), (2, 1), (1, 0)):
        part = slice(0, 2) if t == -1 else slice(0, 4)
        for ref, landing, sems, _, _, s in sides:
            later.append(remote(ref.at[part], landing.at[n, part], sems, n, t, s))
    send_vel = remote(vel_n, vel_f, v_sem, 0, -1, 0)
    send_x = [remote(gf_v, gr_1, g_sem, 0, 1, 0),
              remote(xs_p, xr_m, x_sem, 0, 1, 0),
              remote(gf_v.at[:, CELLS - NZ:, :], gr_2, g_sem, 1, 2, 0),
              remote(xs_n, xr_p, x_sem, 1, -1, 0)]
    for copy in later + [send_vel, send_x[1], send_x[3], send_x[2], send_x[0]]:
        copy.start()

    def interpolated(table, b):
        spot, row = place(b)
        frac = frac_v[pl.ds(b * 8, 8), :]
        rest = 1.0 - frac
        found = [jnp.zeros((8, MK), F32) for _ in range(3)]
        for r in range(CELLS):
            weight = jnp.where(row == r, rest, jnp.where(row == r - 1, frac, 0.0))
            for c in range(3):
                line = jnp.broadcast_to(table[c, r:r + 1, :], (8, TY))
                found[c] = found[c] + weight * jnp.take_along_axis(line, spot, axis=1)
        return found

    def near_step(b, carry):
        for c, found in enumerate(interpolated(vel_n, b)):
            mf_v[c, pl.ds(b * 8, 8), :] = STIFFNESS * (blade_v[c, pl.ds(b * 8, 8), :] - found)
        return carry

    def far_step(b, carry):
        far = side_v[pl.ds(b * 8, 8), :] == 1
        for c, found in enumerate(interpolated(vel_f, b)):
            force = STIFFNESS * (blade_v[c, pl.ds(b * 8, 8), :] - found)
            mf_v[c, pl.ds(b * 8, 8), :] = jnp.where(far, force, mf_v[c, pl.ds(b * 8, 8), :])
        return carry

    lax.fori_loop(0, BL // 8, near_step, 0, unroll=4)
    send_vel.wait()
    lax.fori_loop(0, BL // 8, far_step, 0, unroll=4)
    for copy in send_x:
        copy.wait()

    force = {}
    for x in range(-1, TX + 1):
        if x == -1:
            fields = [gr_2[n] for n in range(5)]
            vel = [xr_m[5 + c] for c in range(3)]
        elif x == TX:
            fields = [gf_v[n, rows(0), :] for n in range(5)]
            vel = [xr_p[5 + c] for c in range(3)]
        else:
            fields = [gr_1[n, rows(x), :] for n in range(5)]
            vel = [vel_n[c, rows(x), :] for c in range(3)]
        force[x] = force_of(fields, vel, 0)

    _, plane = lanes_and_planes()

    def post_at(i, x):
        if x == -1:
            value = xr_m[XP.index(i)]
        elif x == TX:
            value = xr_p[XN.index(i)]
        else:
            value = post_v[i, rows(x), :]
        push = pushed(i, force[x])
        return value if push is None else value + push

    def moved(i, x):
        value = post_at(i, x)
        cy = VELOCITIES[i][1]
        return value if cy == 0 else pltpu.roll(value, cy % TY, 1)

    for x in range(TX):
        for i in range(19):
            cx, _, cz = VELOCITIES[i]
            value = moved(i, x - cx)
            if cz == 1:
                value = jnp.where(plane == 0, post_at(opposite_of(i), x), pltpu.roll(value, 1, 0))
            elif cz == -1:
                value = jnp.where(plane == NZ - 1, moved(mirror_of(i), x - cx), pltpu.roll(value, NZ - 1, 0))
            new_v[i, planes(x), :] = value

    for copy in send_y + later:
        copy.wait_send()
    for copy in later + send_y:
        copy.wait_recv()


def finish(mid, mf, yr_p, yr_n, new_v, mf_v):
    for i in range(19):
        if VELOCITIES[i][1] == 0:
            new_v[i] = mid[i]
    mf_v[...] = mf[...]
    lane, plane = lanes_and_planes()

    row = lax.broadcasted_iota(jnp.int32, (4, TY), 0)

    def source(first, second):
        return jnp.concatenate([jnp.where(row < 2, ref[first], ref[second]) for ref in (yr_p, yr_n)], axis=0)

    before, own, after = source(2, 3), source(1, 2), source(0, 1)
    lines = []
    for g in range(4):
        turn = TY - 4 * NZ * g
        line = jnp.where(lane < NZ, pltpu.roll(before, (turn - 3 * NZ) % TY, 1),
                         jnp.where(lane < 5 * NZ, pltpu.roll(own, (turn + NZ) % TY, 1),
                                   pltpu.roll(after, (turn + 5 * NZ) % TY, 1)))
        lines.append(jnp.where(lane < 6 * NZ, line, 0.0))
    edges = {}
    for n, group in enumerate((YP, YN)):
        line = [lines[q % 4][4 * n + q // 4:4 * n + q // 4 + 1, :] for q in range(13)]
        force = force_of(line[8:], line[5:8], 1)
        for q, i in enumerate(group):
            edges[i] = line[q] + pushed(i, force)

    columns = {}

    def column(i, x):
        if (i, x) not in columns:
            spot = lane == plane + (x + 1) * NZ
            column = jnp.sum(jnp.where(spot, jnp.broadcast_to(edges[i], (NZ, TY)), 0.0), axis=1, keepdims=True)
            columns[i, x] = jnp.broadcast_to(column, (NZ, TY))
        return columns[i, x]

    for i in YP + YN:
        cx, cy, cz = VELOCITIES[i]
        here = lane == (0 if cy == 1 else TY - 1)
        for x in range(TX):
            value = column(i, x - cx)
            where = here
            if cz == 1:
                value = pltpu.roll(value, 1, 0)
                where = jnp.logical_and(here, plane > 0)
            elif cz == -1:
                value = jnp.where(plane == NZ - 1, column(mirror_of(i), x - cx), pltpu.roll(value, NZ - 1, 0))
            new_v[i, planes(x), :] = jnp.where(where, value, mid[i, planes(x), :])


def local(dist, marker_cell, marker_side, marker_frac, blade_vel):
    hbm = pl.BlockSpec(memory_space=pltpu.HBM)
    vmem = pl.BlockSpec(memory_space=pltpu.VMEM)
    cells = pltpu.VMEM((19, CELLS, TY), F32)
    field = pltpu.VMEM((3, CELLS, TY), F32)
    edge = pltpu.VMEM((4, TY), F32)
    dma = pltpu.SemaphoreType.DMA
    shape = jax.ShapeDtypeStruct
    given = [pltpu.with_memory_space_constraint(a, pltpu.HBM) for a in (
        dist.reshape(19, CELLS, TY), marker_cell, marker_side, marker_frac, blade_vel)]
    mid, mf, yr_p, yr_n = pl.pallas_call(
        exchange,
        out_shape=(shape((19, CELLS, TY), F32), shape((3, BL, MK), F32),
                   shape((4, 4, TY), F32), shape((4, 4, TY), F32)),
        in_specs=[hbm] * 5,
        out_specs=(vmem,) * 4,
        scratch_shapes=[
            cells, pltpu.VMEM((BL, MK), jnp.int32), pltpu.VMEM((BL, MK), jnp.int32), pltpu.VMEM((BL, MK), F32),
            pltpu.VMEM((3, BL, MK), F32),
            field, field, cells, pltpu.VMEM((8, NZ, TY), F32), pltpu.VMEM((8, NZ, TY), F32),
            pltpu.VMEM((8, NZ, TY), F32), pltpu.VMEM((8, NZ, TY), F32),
            pltpu.VMEM((5, CELLS, TY), F32), pltpu.VMEM((5, CELLS, TY), F32), pltpu.VMEM((5, CELLS, TY), F32), pltpu.VMEM((5, NZ, TY), F32),
            edge, edge,
            dma((5,)), dma((2, 1)), dma((2, 2)), dma((2, 2)), dma((2, 4)), dma((2, 4)),
        ],
        compiler_params=pltpu.CompilerParams(collective_id=0, has_side_effects=True, vmem_limit_bytes=32 * 2**20),
        name="exchange",
    )(*given)
    new, force = pl.pallas_call(
        finish,
        out_shape=(shape((19, CELLS, TY), F32), shape((3, BL, MK), F32)),
        in_specs=[vmem] * 4,
        out_specs=(vmem, vmem),
        compiler_params=pltpu.CompilerParams(vmem_limit_bytes=16 * 2**20),
        name="finish",
    )(mid, mf, yr_p, yr_n)
    return new.reshape(dist.shape), force


def solution(mesh):
    return jax.shard_map(
        local,
        mesh=mesh,
        in_specs=(
            P(None, None, "gx", "gy"),
            P(("gx", "gy"), None),
            P(("gx", "gy"), None),
            P(("gx", "gy"), None),
            P(None, ("gx", "gy"), None),
        ),
        out_specs=(P(None, None, "gx", "gy"), P(None, ("gx", "gy"), None)),
        check_vma=False,
    )
```
